32 devices in a mesh: ens: 2 (over y), space: 4 (over z), tm: 2 (over x), spin: 2 (over core).
Axes of the slice: x: 2, y: 2, z: 4, core: 2. Of those that a mesh axis runs over, the one named last changes fastest.
Arguments:
- eigvecs: bfloat16 [4, 2, 3, 8192, 128], P('tm', None, None, 'space'), may hold values from -6 to 6
- links: bfloat16 [4, 3, 2, 3, 3, 8192], P('tm', None, None, None, None, 'space'), may hold values from -2.5 to 2.5
- directions: int32 [4], P('spin'), may hold values from 0 to 3, each once
- pair_list: int32 [32, 2], P(('space', 'tm')), may hold values from 0 to 3
- pair_operators: int32 [32, 2], P(('space', 'tm')), may hold values from 0 to 3
- perambulators: bfloat16 [32, 16, 2, 128, 128], P(('space', 'tm'), 'spin'), may hold values from -0.5 to 0.5
Outputs:
- elementals: float32 [8, 4, 128, 2, 128], P(('ens', 'tm'), 'spin', 'space'), parts along dimension 0
- correlators: float32 [64, 2], P(('ens', 'space', 'tm')), parts along dimension 0
The draws below stay inside these ranges and needn't reach their ends.
There are 2 independent parts, one for each index of `ens`. The reference program is written for one: setup_inputs(seed, part) draws one part's arguments, and reference() takes and returns one part's arrays. A program takes and returns all parts, laid end to end along the dimension named above; an argument that names none is the same for every part. Nothing has to cross between parts.
Inputs may be any that keep to these rules, and one draw needn't show every extreme that they name: `directions`: each code once; 0, 1, 2 name a covariant derivative along the first, second and third spatial direction, 3 the eigenvectors with one unit of momentum along the third.
All inputs are finite; a program needn't handle non-finite values.
Results may differ from the reference program's by a relative error of at most 0.0071.
Values may be sent and summed in bfloat16 or wider, within the bound.
No kernel may reach another device: no remote copies, remote signals or barrier semaphores. Data moves between devices by JAX's collectives and lax.ppermute only.
A program may use at most 128 MiB of HBM per device.

```python
import math
from functools import partial
import jax
import jax.numpy as jnp
from jax import lax

NEV = 128
SPIN_PAIRS = 16
NOPS = 4
PX = 16
PY = 16
ZB = 8
NT = 4
NSITES = 8192
NP = 32
N_SPACE = 4


def touch_ends(entries, stream_key, low, top_value):
    longest = entries.shape.index(max(entries.shape))
    spots = []
    for shift in (0, 1):
        where = [jax.random.randint(jax.random.fold_in(stream_key, axis), (), 0, length) for axis, length in enumerate(entries.shape)]
        where[longest] = (where[longest] + shift) % entries.shape[longest]
        spots.append(tuple(where))
    return entries.at[spots[0]].set(low).at[spots[1]].set(top_value)


def level_of(stream_key, shape, shards, smallest, top_value):
    def one(dim, blocks):
        draws = jax.random.uniform(jax.random.fold_in(jax.random.fold_in(stream_key, 6), dim), (blocks,), jnp.float32, smallest / len(shards), top_value / len(shards))
        return jnp.repeat(jnp.exp(draws), shape[dim] // blocks).reshape((-1,) + (1,) * (len(shape) - dim - 1))

    level = one(*shards[0])
    for cut in shards[1:]:
        level = level * one(*cut)
    return level


def centred(key, extent, width, reach, shards=(), held_as=jnp.bfloat16):
    loudness = level_of(key, extent, shards, -0.22, 0.18) if shards else 1.0
    entries = jax.random.normal(key, extent, jnp.float32) * width * loudness
    return jnp.minimum(jnp.maximum(entries, -reach), reach).astype(held_as)


def setup_inputs(seed: int = 0, part: int = 0) -> dict:
    seeds = jax.random.split(jax.random.key(seed), 7)
    return {
        "eigvecs": centred(seeds[0], (NT, 2, 3, NSITES, NEV), 1.0, 6.0, ((0, 2), (3, 4))),
        "links": centred(seeds[1], (NT, 3, 2, 3, 3, NSITES), 0.4, 2.5, ((0, 2), (5, 4))),
        "directions": jax.random.permutation(seeds[2], NOPS).astype(jnp.int32),
        "pair_list": touch_ends(jax.random.randint(seeds[3], (NP, 2), 0, NT), jax.random.fold_in(seeds[3], 1), 0, NT - 1).astype(jnp.int32),
        "pair_operators": touch_ends(jax.random.randint(seeds[4], (NP, 2), 0, NOPS), jax.random.fold_in(seeds[4], 1), 0, NOPS - 1).astype(jnp.int32),
        "perambulators": centred(seeds[5], (NP, SPIN_PAIRS, 2, NEV, NEV), NEV ** -0.5, 0.5, ((0, 8), (1, 2))),
    }


def apply_links(link_field, vectors):
    for b in range(3):
        link_real = link_field[0, :, b][..., None]
        link_imag = link_field[1, :, b][..., None]
        term_real = link_real * vectors[0, b] - link_imag * vectors[1, b]
        term_imag = link_real * vectors[1, b] + link_imag * vectors[0, b]
        if b == 0:
            total_real, total_imag = (term_real, term_imag)
        else:
            total_real, total_imag = (total_real + term_real, total_imag + term_imag)
    return jnp.stack([total_real, total_imag])

def apply_adjoint(link_field, vectors):
    for b in range(3):
        link_real = link_field[0, b][..., None]
        link_imag = link_field[1, b][..., None]
        term_real = link_real * vectors[0, b] + link_imag * vectors[1, b]
        term_imag = link_real * vectors[1, b] - link_imag * vectors[0, b]
        if b == 0:
            total_real, total_imag = (term_real, term_imag)
        else:
            total_real, total_imag = (total_real + term_real, total_imag + term_imag)
    return jnp.stack([total_real, total_imag])

def phase_field(vectors, z_coord, z_total):
    angles = 2.0 * math.pi / z_total * z_coord
    cosine_part = jnp.cos(angles)[:, None, None, None]
    sine_part = jnp.sin(angles)[:, None, None, None]
    return jnp.stack([cosine_part * vectors[0] + sine_part * vectors[1], cosine_part * vectors[1] - sine_part * vectors[0]])

def covariant(direction, vectors, link_field):
    roll_axis = 4 - direction
    links_along = link_field[direction]
    forward = apply_links(links_along, jnp.roll(vectors, -1, roll_axis))
    backward = jnp.roll(apply_adjoint(links_along, vectors), 1, roll_axis)
    return 0.5 * (forward - backward)

def gram_block(vectors_half, displaced, scaling):
    columns = vectors_half.shape[-1]
    left_side = vectors_half.reshape(-1, columns)
    displaced_half = displaced.astype(jnp.bfloat16)
    field_real = displaced_half[0].reshape(-1, columns)
    field_imag = displaced_half[1].reshape(-1, columns)
    right_side = jnp.concatenate([jnp.concatenate([field_real, field_imag], 0), jnp.concatenate([field_imag, -field_real], 0)], 1)
    product = lax.dot_general(left_side, right_side, (((0,), (0,)), ((), ())), preferred_element_type=jnp.float32)
    return (product * scaling).reshape(columns, 2, columns)

def contract_pair(source, sink_matrix, blocks, pair_signs):
    columns = source.shape[-1]
    sink_block = jnp.concatenate([jnp.concatenate([sink_matrix[:, 0], -sink_matrix[:, 1]], 1), jnp.concatenate([sink_matrix[:, 1], sink_matrix[:, 0]], 1)], 0)
    source_block = jnp.concatenate([jnp.concatenate([source[:, 0], source[:, 1]], 1), jnp.concatenate([-source[:, 1], source[:, 0]], 1)], 0)
    source_block = source_block.reshape(2, columns, 2 * columns)
    stacked = blocks.reshape(blocks.shape[0], 2 * columns, columns)
    halfway = jnp.einsum('mk,qkn->qmn', sink_block.astype(jnp.float32), stacked.astype(jnp.float32)).astype(jnp.bfloat16)
    second = jnp.einsum('qcmk,ckn->qmn', halfway.reshape(-1, 2, columns, columns).astype(jnp.float32), source_block.astype(jnp.float32))
    tau_real = blocks[:, 0].astype(jnp.float32)
    tau_imag = blocks[:, 1].astype(jnp.float32)
    out_real = second[:, :, :columns]
    out_imag = second[:, :, columns:]
    trace_real = lax.optimization_barrier(jnp.sum(out_real * tau_real + out_imag * tau_imag, axis=(1, 2)))
    trace_imag = lax.optimization_barrier(jnp.sum(out_imag * tau_real - out_real * tau_imag, axis=(1, 2)))
    return jnp.stack([jnp.sum(pair_signs * trace_real), jnp.sum(pair_signs * trace_imag)]) / (4.0 * columns)

def reference(eigvecs, links, directions, pair_list, pair_operators, perambulators):
    z_total = ZB * N_SPACE
    scaling = 1.0 / math.sqrt(6.0 * PX * PY * z_total)
    z_coord = jnp.arange(z_total).astype(jnp.float32)
    branches = [partial(covariant, 0), partial(covariant, 1), partial(covariant, 2), lambda vectors, link_field: phase_field(vectors, z_coord, z_total)]

    def per_slice(inputs):
        vectors_half, link_half = inputs
        vectors = vectors_half.astype(jnp.float32).reshape(2, 3, z_total, PY, PX, NEV)
        link_field = link_half.astype(jnp.float32).reshape(3, 2, 3, 3, z_total, PY, PX)
        blocks = []
        for op_slot in range(NOPS):
            displaced = lax.switch(directions[op_slot], branches, vectors, link_field)
            blocks.append(gram_block(vectors_half, displaced, scaling))
        return jnp.stack(blocks)
    elementals = lax.map(per_slice, (eigvecs, links))
    halves = elementals.astype(jnp.bfloat16)
    spin_signs = jnp.where(jnp.arange(4) < 2, 1.0, -1.0).astype(jnp.float32)
    pair_signs = (spin_signs[:, None] * spin_signs[None, :]).reshape(SPIN_PAIRS)

    def per_pair(inputs):
        time_pair, operator_pair, blocks = inputs
        source = halves[time_pair[0], operator_pair[0]]
        sink_matrix = halves[time_pair[1], operator_pair[1]]
        return contract_pair(source, sink_matrix, blocks, pair_signs)
    correlators = lax.map(per_pair, (pair_list, pair_operators, perambulators))
    return (elementals, correlators)
```

```python
from functools import partial
import math

import jax
import jax.numpy as jnp
from jax import lax
from jax.experimental import pallas as pl
from jax.experimental.pallas import tpu as pltpu
from jax.sharding import PartitionSpec as P

PX = 16
PY = 16
LANES = 128
ROWS = 8


def flip(array, axis, mask):
    count = lax.axis_size(axis)
    return lax.ppermute(array, axis, [(i, i ^ mask) for i in range(count)])


def flip_both(array, space_mask, tm_mask):
    space, tm = lax.axis_size("space"), lax.axis_size("tm")
    pairs = [
        (z * tm + x, (z ^ space_mask) * tm + (x ^ tm_mask)) for z in range(space) for x in range(tm)
    ]
    return lax.ppermute(array, ("space", "tm"), pairs)


def transposed_plane(v_ref, vt_ref):
    for part in range(2):
        for colour in range(3):
            vt_ref[3 * part + colour] = v_ref[part, colour].astype(jnp.float32).T


def stacked_plane(v_ref, vr_ref, shift=0):
    sites = v_ref.shape[2]
    for part in range(2):
        columns = slice(part * LANES, (part + 1) * LANES)
        for colour in range(3):
            start = colour * sites
            if shift:
                vr_ref[start : start + shift, columns] = v_ref[part, colour, sites - shift :]
            vr_ref[start + shift : start + sites, columns] = v_ref[part, colour, : sites - shift]


def permuted_plane(v_ref, vr_ref, permutation):
    sites = v_ref.shape[2]
    for colour in range(3):
        plane = jnp.concatenate([v_ref[0, colour], v_ref[1, colour]], 1)
        vr_ref[colour * sites : (colour + 1) * sites] = dot(permutation, plane).astype(jnp.bfloat16)


def link_sums(u, uf_ref):
    real, imag = u[..., 0:1, :], u[..., 1:2, :]
    uf_ref[..., 0:1, :] = real
    uf_ref[..., 1:2, :] = imag - real
    uf_ref[..., 2:3, :] = imag + real


def turned(u, amount):
    sites = u.shape[-1]
    return jnp.concatenate([u[..., sites - amount :], u[..., : sites - amount]], -1)


def link_rows(uf_ref, lead, lanes):
    return [
        [[uf_ref[lead + (a, b, slice(i, i + 1), lanes)] for b in range(3)] for a in range(3)]
        for i in range(3)
    ]


def times_links(rows, vectors, f_ref, k_tile, lanes, sites):
    sums = [vectors[0][b] + vectors[1][b] for b in range(3)]
    for a in range(3):
        k1 = sum_products(rows[0][a], sums)
        k2 = sum_products(rows[1][a], vectors[0])
        k3 = sum_products(rows[2][a], vectors[1])
        for part, value in ((0, k1 - k3), (1, k1 + k2)):
            start = part * LANES + k_tile * ROWS
            high = value.astype(jnp.bfloat16)
            low = (value - high.astype(jnp.float32)).astype(jnp.bfloat16)
            columns = slice(a * sites + lanes.start, a * sites + lanes.stop)
            for copy, piece in ((0, high), (1, low)):
                at = copy * 2 * LANES + start
                f_ref[at : at + ROWS, columns] = piece


def direction(rows_of, vt, f_ref):
    sites = vt.shape[2]
    for j in range(sites // LANES):
        lanes = slice(j * LANES, (j + 1) * LANES)
        rows = rows_of(lanes)
        for k_tile in range(LANES // ROWS):
            k = slice(k_tile * ROWS, (k_tile + 1) * ROWS)
            vectors = [[vt[3 * part + c, k, lanes] for c in range(3)] for part in range(2)]
            times_links(rows, vectors, f_ref, k_tile, lanes, sites)


def gram(f_ref, vr_ref):
    both = dot(f_ref[...], vr_ref[...])
    return both[: 2 * LANES] + both[2 * LANES :]


def sum_products(left, right):
    return left[0] * right[0] + left[1] * right[1] + left[2] * right[2]


def block(acc, q, p):
    return acc[q * LANES : (q + 1) * LANES, p * LANES : (p + 1) * LANES]


def upper(shape):
    row = lax.broadcasted_iota(jnp.int32, shape, 0)
    column = lax.broadcasted_iota(jnp.int32, shape, 1)
    return row <= column


def antihermitian(acc, scale):
    real = block(acc, 0, 0) + block(acc, 1, 1)
    imag = block(acc, 1, 0) - block(acc, 0, 1)
    e_real = scale * (real.T - real)
    e_imag = scale * (imag.T + imag)
    return jnp.where(upper(real.shape), e_imag, e_real)


def dot(left, right):
    return jnp.dot(left, right, preferred_element_type=jnp.float32)


def store_halves(out_ref, at, matrix, parity):
    half_rows = matrix.shape[0] // 2
    for half in range(2):
        out_ref[parity ^ half, at] = matrix[half * half_rows : (half + 1) * half_rows]


def plane_kernel(
    where_ref, v_ref, u_ref, below_ref, out_ref, inner_ref, waves, vt, vtb, vr, vx, vy, vz, uf, f0, f1, f2, acc, *, scale, step
):
    plane = pl.program_id(0)
    planes = pl.num_programs(0)
    sites = v_ref.shape[2]

    @pl.when(plane == 0)
    def _():
        acc[...] = jnp.zeros_like(acc)
        waves[...] = jnp.zeros_like(waves)
        vr[...] = jnp.zeros_like(vr)
        vz[...] = jnp.zeros_like(vz)
        f2[...] = jnp.zeros_like(f2)

    acc[2] += gram(f2, vz)
    vz[...] = vr[...]

    column = lax.broadcasted_iota(jnp.int32, (sites, sites), 1)
    row = lax.broadcasted_iota(jnp.int32, (sites, sites), 0)
    before = row - row % PX + (row + PX - 1) % PX
    permutation = jnp.where(column == before, 1.0, 0.0).astype(jnp.bfloat16)
    transposed_plane(v_ref, vt)
    stacked_plane(v_ref, vr)
    stacked_plane(v_ref, vy, PX)
    permuted_plane(v_ref, vx, permutation)

    u0 = u_ref[0].astype(jnp.float32)
    lane = lax.broadcasted_iota(jnp.int32, u0.shape, 3)
    link_sums(jnp.where(lane % PX == 0, turned(u0, sites - PX + 1), turned(u0, 1)), uf.at[0])
    link_sums(turned(u_ref[1].astype(jnp.float32), PX), uf.at[1])
    link_sums(below_ref[...].astype(jnp.float32), uf.at[2])

    direction(partial(link_rows, uf, (0,)), vt, f0)
    for part in range(2):
        for colour in range(3):
            vtb[part * LANES : (part + 1) * LANES, colour * sites : (colour + 1) * sites] = vt[
                3 * part + colour
            ].astype(jnp.bfloat16)
    own = dot(vtb[...], vr[...])
    g_real = block(own, 0, 0) + block(own, 1, 1)
    g_imag = block(own, 0, 1) - block(own, 1, 0)
    packed = jnp.where(upper(g_real.shape), g_real, g_imag)
    z = where_ref[1] * planes + plane
    angle = step * jnp.full((8, LANES), z, jnp.int32).astype(jnp.float32)
    waves[0] += jnp.cos(angle)[0:1] * packed
    waves[1] += jnp.sin(angle)[0:1] * packed

    acc[0] += gram(f0, vx)
    direction(partial(link_rows, uf, (1,)), vt, f1)
    acc[1] += gram(f1, vy)
    direction(partial(link_rows, uf, (2,)), vt, f2)

    @pl.when(plane == planes - 1)
    def _():
        parity = where_ref[1] % 2
        cos_sym, cos_anti = unpack(scale * waves[0])
        sin_sym, sin_anti = unpack(scale * waves[1])
        store_halves(out_ref, 0, antihermitian(acc[0], 0.5 * scale), parity)
        store_halves(out_ref, 1, antihermitian(acc[1], 0.5 * scale), parity)
        store_halves(out_ref, 2, cos_sym + sin_anti, parity)
        store_halves(out_ref, 3, cos_anti - sin_sym, parity)
        inner_ref[...] = antihermitian(acc[2] + gram(f2, vz), 0.5 * scale)


def rim_kernel(where_ref, v_ref, halo_ref, u_ref, inner_ref, out_ref, vt, vr, uf, f2, *, scale):
    link_sums(u_ref[...].astype(jnp.float32), uf)
    transposed_plane(halo_ref, vt)
    stacked_plane(v_ref, vr)
    direction(partial(link_rows, uf, ()), vt, f2)
    total = inner_ref[...] + antihermitian(gram(f2, vr), 0.5 * scale)
    store_halves(out_ref, 0, total, where_ref[1] % 2)


def unpack(packed):
    flipped = packed.T
    row = lax.broadcasted_iota(jnp.int32, packed.shape, 0)
    column = lax.broadcasted_iota(jnp.int32, packed.shape, 1)
    symmetric = jnp.where(row <= column, packed, flipped)
    antisymmetric = jnp.where(row > column, packed, jnp.where(row < column, -flipped, 0.0))
    return symmetric, antisymmetric


def round_kernel(mine_a, got_a, mine_b, got_b, out_ref):
    sums = mine_a[...] + got_a[...]
    out_ref[0] = sums[0].astype(jnp.bfloat16)
    out_ref[1] = sums[1].astype(jnp.bfloat16)
    out_ref[2] = (mine_b[0] + got_b[0]).astype(jnp.bfloat16)
    out_ref[3] = sums[2].astype(jnp.bfloat16)
    out_ref[4] = sums[3].astype(jnp.bfloat16)


def elemental(table, slot, code):
    third = code == 3
    packed = table[slot, jnp.where(third, 3, code)].astype(jnp.float32)
    other = table[slot, 4].astype(jnp.float32)
    symmetric, antisymmetric = unpack(packed)
    real = jnp.where(third, packed, antisymmetric)
    imag = jnp.where(third, other, symmetric)
    return real, imag


def fill(table, where_ref, parts):
    half_rows = table.shape[2] // 2
    parity = where_ref[1] % 2
    for at, halves in enumerate(parts):
        for i, half in enumerate(halves):
            start = pl.multiple_of((parity ^ i) * half_rows, half_rows)
            table[at, :, pl.ds(start, half_rows), :] = half[...]


def slot_of(where_ref, slice_index, tm_size):
    spin_size = where_ref[3]
    owner = slice_index // spin_size
    within = slice_index % spin_size
    return (within ^ where_ref[0]) * tm_size + (owner ^ where_ref[2])


def pair_kernel(where_ref, codes_ref, pairs_ref, operators_ref, *refs, tm_size, slots, q_count):
    *halves, tau_ref, out_ref, table = refs
    pair = pl.program_id(0)
    columns = LANES

    @pl.when(pair == 0)
    def _():
        fill(table, where_ref, [halves[i : i + 2] for i in range(0, len(halves), 2)])
        out_ref[...] = jnp.zeros_like(out_ref)

    def matrix(end):
        operator = operators_ref[end, pair]
        core = operator // slots
        code = codes_ref[(core ^ where_ref[0]) * slots + operator % slots]
        slot = slot_of(where_ref, pairs_ref[end, pair], tm_size)
        real, imag = elemental(table, slot, code)
        return real.astype(jnp.bfloat16), imag.astype(jnp.bfloat16)

    r_real, r_imag = matrix(0)
    s_real, s_imag = matrix(1)
    sink = jnp.concatenate(
        [
            jnp.concatenate([s_real, -s_imag], 1),
            jnp.concatenate([s_imag, s_real], 1),
        ],
        0,
    )
    source = jnp.concatenate(
        [
            jnp.concatenate([r_real, r_imag], 1),
            jnp.concatenate([-r_imag, r_real], 1),
        ],
        0,
    )
    sum_real = jnp.zeros((columns, columns), jnp.float32)
    sum_imag = jnp.zeros((columns, columns), jnp.float32)
    for q in range(0, q_count, 2):
        pairwise = jnp.concatenate(
            [tau_ref[q + i].reshape(2 * columns, columns) for i in range(2)], 1
        )
        halfway = dot(sink, pairwise)
        left = jnp.concatenate(
            [
                jnp.concatenate(
                    [
                        halfway[:columns, i * columns : (i + 1) * columns],
                        halfway[columns:, i * columns : (i + 1) * columns],
                    ],
                    1,
                )
                for i in range(2)
            ],
            0,
        )
        high = left.astype(jnp.bfloat16)
        low = (left - high.astype(jnp.float32)).astype(jnp.bfloat16)
        second = dot(high, source) + dot(low, source)
        for i in range(2):
            out_real = second[i * columns : (i + 1) * columns, :columns]
            out_imag = second[i * columns : (i + 1) * columns, columns:]
            tau_real = tau_ref[q + i, 0].astype(jnp.float32)
            tau_imag = tau_ref[q + i, 1].astype(jnp.float32)
            spin_pair = where_ref[0] * q_count + q + i
            sign = jnp.where((spin_pair // 4 < 2) == (spin_pair % 4 < 2), 1.0, -1.0)
            sum_real += sign * (out_real * tau_real + out_imag * tau_imag)
            sum_imag += sign * (out_imag * tau_real - out_real * tau_imag)
    total_real = jnp.sum(sum_real) / (4.0 * columns)
    total_imag = jnp.sum(sum_imag) / (4.0 * columns)
    row = lax.broadcasted_iota(jnp.int32, out_ref.shape, 0)
    column = lax.broadcasted_iota(jnp.int32, out_ref.shape, 1)
    total = jnp.where(row == 0, total_real, total_imag)
    out_ref[...] = jnp.where(column == pair, total, out_ref[...])


def elemental_kernel(where_ref, codes_ref, *refs):
    *halves, out_ref, table, rows_ref = refs
    fill(table, where_ref, [halves[i : i + 2] for i in range(0, len(halves), 2)])
    slices, slots, row_count = out_ref.shape[0], out_ref.shape[1], out_ref.shape[2]
    start = pl.multiple_of(where_ref[1] * row_count, row_count)
    for t in range(slices):
        for o in range(slots):
            real, imag = elemental(table, t ^ where_ref[0], codes_ref[o])
            rows_ref[0] = real
            rows_ref[1] = imag
            for part in range(2):
                out_ref[t, o, :, part] = rows_ref[part, pl.ds(start, row_count), :]


def shards(eigvecs, links, directions, pair_list, pair_operators, perambulators):
    slices, _, _, local_sites, columns = eigvecs.shape
    space = lax.axis_size("space")
    tm_size = lax.axis_size("tm")
    spin_size = lax.axis_size("spin")
    assert slices == spin_size and columns == LANES
    sites = PX * PY
    planes = local_sites // sites
    z_total = planes * space
    scale = 1.0 / math.sqrt(6.0 * sites * z_total)
    slots = directions.shape[0]
    pair_count, q_count = perambulators.shape[0], perambulators.shape[1]

    me = lax.axis_index("spin")
    where = jnp.stack(
        [me, lax.axis_index("space"), lax.axis_index("tm"), spin_size]
    ).astype(jnp.int32)
    lowest = lax.dynamic_slice(eigvecs, (me, 0, 0, 0, 0), (1, 2, 3, sites, columns))[0]
    halo = lax.ppermute(lowest, "space", [(i, (i - 1) % space) for i in range(space)])
    halo, other_codes = lax.optimization_barrier((halo, flip(directions, "spin", 1)))
    codes = jnp.concatenate([directions, other_codes])

    params = pltpu.CompilerParams(dimension_semantics=("arbitrary",), vmem_limit_bytes=50 << 20)
    stack_shape = pltpu.VMEM((3 * sites, 2 * LANES), jnp.bfloat16)
    f_shape = pltpu.VMEM((4 * LANES, 3 * sites), jnp.bfloat16)
    vt_shape = pltpu.VMEM((6, LANES, sites), jnp.float32)
    link_field = links.transpose(0, 1, 3, 4, 2, 5)
    estimate = lambda flops: pl.CostEstimate(flops=flops, bytes_accessed=1 << 22, transcendentals=0)
    half_rows = columns // 2
    part_a, inner = pl.pallas_call(
        partial(plane_kernel, scale=scale, step=2.0 * math.pi / z_total),
        out_shape=(
            jax.ShapeDtypeStruct((2, 4, half_rows, columns), jnp.float32),
            jax.ShapeDtypeStruct((columns, columns), jnp.float32),
        ),
        grid_spec=pltpu.PrefetchScalarGridSpec(
            num_scalar_prefetch=1,
            grid=(planes,),
            in_specs=[
                pl.BlockSpec((None, 2, 3, sites, columns), lambda z, w: (w[0], 0, 0, z, 0)),
                pl.BlockSpec((None, 2, 3, 3, 2, sites), lambda z, w: (w[0], 0, 0, 0, 0, z)),
                pl.BlockSpec(
                    (None, None, 3, 3, 2, sites),
                    lambda z, w: (w[0], 2, 0, 0, 0, jnp.maximum(z - 1, 0)),
                ),
            ],
            out_specs=(
                pl.BlockSpec((2, 4, half_rows, columns), lambda z, w: (0, 0, 0, 0)),
                pl.BlockSpec((columns, columns), lambda z, w: (0, 0)),
            ),
            scratch_shapes=[
                pltpu.VMEM((2, columns, columns), jnp.float32),
                vt_shape,
                pltpu.VMEM((2 * LANES, 3 * sites), jnp.bfloat16),
                stack_shape,
                stack_shape,
                stack_shape,
                stack_shape,
                pltpu.VMEM((3, 3, 3, 3, sites), jnp.float32),
                f_shape,
                f_shape,
                f_shape,
                pltpu.VMEM((3, 2 * LANES, 2 * LANES), jnp.float32),
            ],
        ),
        compiler_params=params,
        cost_estimate=estimate(20 * 10**9),
        name="planes",
    )(where, eigvecs, link_field, link_field)

    part_b = pl.pallas_call(
        partial(rim_kernel, scale=scale),
        out_shape=jax.ShapeDtypeStruct((2, 1, half_rows, columns), jnp.float32),
        grid_spec=pltpu.PrefetchScalarGridSpec(
            num_scalar_prefetch=1,
            grid=(1,),
            in_specs=[
                pl.BlockSpec((None, 2, 3, sites, columns), lambda z, w: (w[0], 0, 0, planes - 1, 0)),
                pl.BlockSpec((2, 3, sites, columns), lambda z, w: (0, 0, 0, 0)),
                pl.BlockSpec((None, None, 3, 3, 2, sites), lambda z, w: (w[0], 2, 0, 0, 0, planes - 1)),
                pl.BlockSpec((columns, columns), lambda z, w: (0, 0)),
            ],
            out_specs=pl.BlockSpec((2, 1, half_rows, columns), lambda z, w: (0, 0, 0, 0)),
            scratch_shapes=[
                vt_shape,
                stack_shape,
                pltpu.VMEM((3, 3, 3, sites), jnp.float32),
                f_shape,
            ],
        ),
        compiler_params=params,
        cost_estimate=estimate(2 * 10**9),
        name="rim",
    )(where, eigvecs, halo, link_field, inner)

    got_a = flip(part_a[1], "space", 1)
    got_b = flip(part_b[1], "space", 1)
    part_a, part_b = part_a[0], part_b[0]
    mask = 2
    while mask < space:
        part_a, got_a, part_b = lax.optimization_barrier((part_a, got_a, part_b))
        part_a, part_b = part_a + got_a, part_b + got_b
        got_a, got_b = flip(part_a, "space", mask), flip(part_b, "space", mask)
        mask *= 2

    mine = pl.pallas_call(
        round_kernel,
        out_shape=jax.ShapeDtypeStruct((5, half_rows, columns), jnp.bfloat16),
        compiler_params=pltpu.CompilerParams(vmem_limit_bytes=50 << 20),
        name="round",
    )(part_a, got_a, part_b, got_b)
    own = [mine, flip_both(mine, 1, 0)]
    for m in range(1, tm_size):
        own += [flip_both(mine, 0, m), flip_both(mine, 1, m)]
    other = [flip(half, "spin", 1) for half in own]

    whole = lambda shape: pl.BlockSpec(shape, lambda p, *_: (0,) * len(shape))

    row_count = columns // space
    elementals = pl.pallas_call(
        elemental_kernel,
        out_shape=jax.ShapeDtypeStruct((slices, slots, row_count, 2, columns), jnp.float32),
        grid_spec=pltpu.PrefetchScalarGridSpec(
            num_scalar_prefetch=2,
            grid=(1,),
            in_specs=[whole(mine.shape)] * 4,
            out_specs=whole((slices, slots, row_count, 2, columns)),
            scratch_shapes=[
                pltpu.VMEM((spin_size, 5, columns, columns), jnp.bfloat16),
                pltpu.VMEM((2, columns, columns), jnp.float32),
            ],
        ),
        compiler_params=params,
        name="rows",
    )(where, codes, *own[:2], *other[:2])

    partial_corr = pl.pallas_call(
        partial(pair_kernel, tm_size=tm_size, slots=slots, q_count=q_count),
        out_shape=jax.ShapeDtypeStruct((2, pair_count), jnp.float32),
        grid_spec=pltpu.PrefetchScalarGridSpec(
            num_scalar_prefetch=4,
            grid=(pair_count,),
            in_specs=[whole(mine.shape)] * (2 * len(own))
            + [
                pl.BlockSpec((None, q_count, 2, columns, columns), lambda p, *_: (p, 0, 0, 0, 0)),
            ],
            out_specs=whole((2, pair_count)),
            scratch_shapes=[
                pltpu.VMEM((spin_size * tm_size, 5, columns, columns), jnp.bfloat16)
            ],
        ),
        compiler_params=params,
        name="pairs",
    )(where, codes, pair_list.T, pair_operators.T, *own, *other, perambulators)
    correlators = (partial_corr + flip(partial_corr, "spin", 1)).T

    return elementals, correlators


def solution(mesh):
    return jax.shard_map(
        shards,
        mesh=mesh,
        in_specs=(
            P("tm", None, None, "space", None),
            P("tm", None, None, None, None, "space"),
            P("spin"),
            P(("space", "tm"), None),
            P(("space", "tm"), None),
            P(("space", "tm"), "spin", None, None, None),
        ),
        out_specs=(P(("ens", "tm"), "spin", "space", None, None), P(("ens", "space", "tm"), None)),
        check_vma=False,
    )
```

```python
from functools import partial
import math

import jax
import jax.numpy as jnp
from jax import lax
from jax.experimental import pallas as pl
from jax.experimental.pallas import tpu as pltpu
from jax.sharding import PartitionSpec as P

PX = 16
PY = 16
LANES = 128
ROWS = 8


def flip(array, axis, mask):
    count = lax.axis_size(axis)
    return lax.ppermute(array, axis, [(i, i ^ mask) for i in range(count)])


def flip_both(array, space_mask, tm_mask):
    space, tm = lax.axis_size("space"), lax.axis_size("tm")
    pairs = [
        (z * tm + x, (z ^ space_mask) * tm + (x ^ tm_mask)) for z in range(space) for x in range(tm)
    ]
    return lax.ppermute(array, ("space", "tm"), pairs)


def transposed_plane(v_ref, vt_ref):
    for part in range(2):
        for colour in range(3):
            vt_ref[3 * part + colour] = v_ref[part, colour].astype(jnp.float32).T


def stacked_plane(v_ref, vr_ref, shift=0):
    sites = v_ref.shape[2]
    for part in range(2):
        columns = slice(part * LANES, (part + 1) * LANES)
        for colour in range(3):
            start = colour * sites
            if shift:
                vr_ref[start : start + shift, columns] = v_ref[part, colour, sites - shift :]
            vr_ref[start + shift : start + sites, columns] = v_ref[part, colour, : sites - shift]


def permuted_plane(v_ref, vr_ref, permutation):
    sites = v_ref.shape[2]
    for colour in range(3):
        plane = jnp.concatenate([v_ref[0, colour], v_ref[1, colour]], 1)
        vr_ref[colour * sites : (colour + 1) * sites] = dot(permutation, plane).astype(jnp.bfloat16)


def link_sums(u, uf_ref):
    real, imag = u[..., 0:1, :], u[..., 1:2, :]
    uf_ref[..., 0:1, :] = real
    uf_ref[..., 1:2, :] = imag - real
    uf_ref[..., 2:3, :] = imag + real


def turned(u, amount):
    sites = u.shape[-1]
    return jnp.concatenate([u[..., sites - amount :], u[..., : sites - amount]], -1)


def link_rows(uf_ref, lead, lanes):
    return [
        [[uf_ref[lead + (a, b, slice(i, i + 1), lanes)] for b in range(3)] for a in range(3)]
        for i in range(3)
    ]


def times_links(rows, vectors, f_ref, k_tile, lanes, sites):
    sums = [vectors[0][b] + vectors[1][b] for b in range(3)]
    for a in range(3):
        k1 = sum_products(rows[0][a], sums)
        k2 = sum_products(rows[1][a], vectors[0])
        k3 = sum_products(rows[2][a], vectors[1])
        for part, value in ((0, k1 - k3), (1, k1 + k2)):
            start = part * LANES + k_tile * ROWS
            high = value.astype(jnp.bfloat16)
            low = (value - high.astype(jnp.float32)).astype(jnp.bfloat16)
            columns = slice(a * sites + lanes.start, a * sites + lanes.stop)
            for copy, piece in ((0, high), (1, low)):
                at = copy * 2 * LANES + start
                f_ref[at : at + ROWS, columns] = piece


def direction(rows_of, vt, f_ref):
    sites = vt.shape[2]
    for j in range(sites // LANES):
        lanes = slice(j * LANES, (j + 1) * LANES)
        rows = rows_of(lanes)
        for k_tile in range(LANES // ROWS):
            k = slice(k_tile * ROWS, (k_tile + 1) * ROWS)
            vectors = [[vt[3 * part + c, k, lanes] for c in range(3)] for part in range(2)]
            times_links(rows, vectors, f_ref, k_tile, lanes, sites)


def gram(f_ref, vr_ref):
    both = dot(f_ref[...], vr_ref[...])
    return both[: 2 * LANES] + both[2 * LANES :]


def sum_products(left, right):
    return left[0] * right[0] + left[1] * right[1] + left[2] * right[2]


def block(acc, q, p):
    return acc[q * LANES : (q + 1) * LANES, p * LANES : (p + 1) * LANES]


def upper(shape):
    row = lax.broadcasted_iota(jnp.int32, shape, 0)
    column = lax.broadcasted_iota(jnp.int32, shape, 1)
    return row <= column


def antihermitian(acc, scale):
    real = block(acc, 0, 0) + block(acc, 1, 1)
    imag = block(acc, 1, 0) - block(acc, 0, 1)
    e_real = scale * (real.T - real)
    e_imag = scale * (imag.T + imag)
    return jnp.where(upper(real.shape), e_imag, e_real)


def dot(left, right):
    return jnp.dot(left, right, preferred_element_type=jnp.float32)


def store_halves(out_ref, at, matrix, parity):
    half_rows = matrix.shape[0] // 2
    for half in range(2):
        out_ref[parity ^ half, at] = matrix[half * half_rows : (half + 1) * half_rows]


def plane_kernel(
    where_ref, v_ref, u_ref, below_ref, out_ref, inner_ref, waves, vt, vtb, vr, vx, vy, vz, uf, f0, f1, f2, acc, *, scale, step
):
    plane = pl.program_id(0)
    planes = pl.num_programs(0)
    sites = v_ref.shape[2]

    @pl.when(plane == 0)
    def _():
        acc[...] = jnp.zeros_like(acc)
        waves[...] = jnp.zeros_like(waves)
        vr[...] = jnp.zeros_like(vr)
        vz[...] = jnp.zeros_like(vz)
        f2[...] = jnp.zeros_like(f2)

    acc[2] += gram(f2, vz)
    vz[...] = vr[...]

    column = lax.broadcasted_iota(jnp.int32, (sites, sites), 1)
    row = lax.broadcasted_iota(jnp.int32, (sites, sites), 0)
    before = row - row % PX + (row + PX - 1) % PX
    permutation = jnp.where(column == before, 1.0, 0.0).astype(jnp.bfloat16)
    transposed_plane(v_ref, vt)
    stacked_plane(v_ref, vr)
    stacked_plane(v_ref, vy, PX)
    permuted_plane(v_ref, vx, permutation)

    u0 = u_ref[0].astype(jnp.float32)
    lane = lax.broadcasted_iota(jnp.int32, u0.shape, 3)
    link_sums(jnp.where(lane % PX == 0, turned(u0, sites - PX + 1), turned(u0, 1)), uf.at[0])
    link_sums(turned(u_ref[1].astype(jnp.float32), PX), uf.at[1])
    link_sums(below_ref[...].astype(jnp.float32), uf.at[2])

    direction(partial(link_rows, uf, (0,)), vt, f0)
    for part in range(2):
        for colour in range(3):
            vtb[part * LANES : (part + 1) * LANES, colour * sites : (colour + 1) * sites] = vt[
                3 * part + colour
            ].astype(jnp.bfloat16)
    own = dot(vtb[...], vr[...])
    g_real = block(own, 0, 0) + block(own, 1, 1)
    g_imag = block(own, 0, 1) - block(own, 1, 0)
    packed = jnp.where(upper(g_real.shape), g_real, g_imag)
    z = where_ref[1] * planes + plane
    angle = step * jnp.full((8, LANES), z, jnp.int32).astype(jnp.float32)
    waves[0] += jnp.cos(angle)[0:1] * packed
    waves[1] += jnp.sin(angle)[0:1] * packed

    acc[0] += gram(f0, vx)
    direction(partial(link_rows, uf, (1,)), vt, f1)
    acc[1] += gram(f1, vy)
    direction(partial(link_rows, uf, (2,)), vt, f2)

    @pl.when(plane == planes - 1)
    def _():
        parity = where_ref[1] % 2
        cos_sym, cos_anti = unpack(scale * waves[0])
        sin_sym, sin_anti = unpack(scale * waves[1])
        store_halves(out_ref, 0, antihermitian(acc[0], 0.5 * scale), parity)
        store_halves(out_ref, 1, antihermitian(acc[1], 0.5 * scale), parity)
        store_halves(out_ref, 2, cos_sym + sin_anti, parity)
        store_halves(out_ref, 3, cos_anti - sin_sym, parity)
        inner_ref[...] = antihermitian(acc[2] + gram(f2, vz), 0.5 * scale)


def rim_kernel(where_ref, v_ref, halo_ref, u_ref, inner_ref, out_ref, vt, vr, uf, f2, *, scale):
    link_sums(u_ref[...].astype(jnp.float32), uf)
    transposed_plane(halo_ref, vt)
    stacked_plane(v_ref, vr)
    direction(partial(link_rows, uf, ()), vt, f2)
    total = inner_ref[...] + antihermitian(gram(f2, vr), 0.5 * scale)
    store_halves(out_ref, 0, total, where_ref[1] % 2)


def unpack(packed):
    flipped = packed.T
    row = lax.broadcasted_iota(jnp.int32, packed.shape, 0)
    column = lax.broadcasted_iota(jnp.int32, packed.shape, 1)
    symmetric = jnp.where(row <= column, packed, flipped)
    antisymmetric = jnp.where(row > column, packed, jnp.where(row < column, -flipped, 0.0))
    return symmetric, antisymmetric


def round_kernel(mine_a, got_a, mine_b, got_b, out_ref):
    sums = mine_a[...] + got_a[...]
    out_ref[0] = sums[0].astype(jnp.bfloat16)
    out_ref[1] = sums[1].astype(jnp.bfloat16)
    out_ref[2] = (mine_b[0] + got_b[0]).astype(jnp.bfloat16)
    out_ref[3] = sums[2].astype(jnp.bfloat16)
    out_ref[4] = sums[3].astype(jnp.bfloat16)


def elemental(table, slot, code):
    third = code == 3
    packed = table[slot, jnp.where(third, 3, code)].astype(jnp.float32)
    other = table[slot, 4].astype(jnp.float32)
    symmetric, antisymmetric = unpack(packed)
    real = jnp.where(third, packed, antisymmetric)
    imag = jnp.where(third, other, symmetric)
    return real, imag


def fill(table, where_ref, parts):
    half_rows = table.shape[2] // 2
    parity = where_ref[1] % 2
    for at, halves in enumerate(parts):
        for i, half in enumerate(halves):
            start = pl.multiple_of((parity ^ i) * half_rows, half_rows)
            table[at, :, pl.ds(start, half_rows), :] = half[...]


def slot_of(where_ref, slice_index, tm_size):
    spin_size = where_ref[3]
    owner = slice_index // spin_size
    within = slice_index % spin_size
    return (within ^ where_ref[0]) * tm_size + (owner ^ where_ref[2])


def folded(values):
    return jnp.sum(values.reshape(-1, 8, values.shape[1]), axis=0)


def pair_kernel(where_ref, codes_ref, pairs_ref, operators_ref, *refs, tm_size, slots, q_count):
    *halves, tau_ref, out_ref, table = refs
    pair = pl.program_id(0)
    columns = LANES

    @pl.when(pair == 0)
    def _():
        fill(table, where_ref, [halves[i : i + 2] for i in range(0, len(halves), 2)])
        out_ref[...] = jnp.zeros_like(out_ref)

    def matrix(end):
        operator = operators_ref[end, pair]
        core = operator // slots
        code = codes_ref[(core ^ where_ref[0]) * slots + operator % slots]
        slot = slot_of(where_ref, pairs_ref[end, pair], tm_size)
        real, imag = elemental(table, slot, code)
        return real.astype(jnp.bfloat16), imag.astype(jnp.bfloat16)

    r_real, r_imag = matrix(0)
    s_real, s_imag = matrix(1)
    sink = jnp.concatenate(
        [
            jnp.concatenate([s_real, -s_imag], 1),
            jnp.concatenate([s_imag, s_real], 1),
        ],
        0,
    )
    source = jnp.concatenate(
        [
            jnp.concatenate([r_real, r_imag], 1),
            jnp.concatenate([-r_imag, r_real], 1),
        ],
        0,
    )
    twice = jnp.concatenate([source, source], 0)
    sum_real = jnp.zeros((8, columns), jnp.float32)
    sum_imag = jnp.zeros((8, columns), jnp.float32)
    for q in range(0, q_count, 2):
        pairwise = jnp.concatenate(
            [tau_ref[q + i].reshape(2 * columns, columns) for i in range(2)], 1
        )
        halfway = dot(sink, pairwise)
        left = jnp.concatenate(
            [
                jnp.concatenate(
                    [
                        halfway[:columns, i * columns : (i + 1) * columns],
                        halfway[columns:, i * columns : (i + 1) * columns],
                    ],
                    1,
                )
                for i in range(2)
            ],
            0,
        )
        high = left.astype(jnp.bfloat16)
        low = (left - high.astype(jnp.float32)).astype(jnp.bfloat16)
        second = dot(jnp.concatenate([high, low], 1), twice)
        for i in range(2):
            out_real = second[i * columns : (i + 1) * columns, :columns]
            out_imag = second[i * columns : (i + 1) * columns, columns:]
            tau_real = tau_ref[q + i, 0].astype(jnp.float32)
            tau_imag = tau_ref[q + i, 1].astype(jnp.float32)
            spin_pair = where_ref[0] * q_count + q + i
            sign = jnp.where((spin_pair // 4 < 2) == (spin_pair % 4 < 2), 1.0, -1.0)
            sum_real += sign * folded(out_real * tau_real + out_imag * tau_imag)
            sum_imag += sign * folded(out_imag * tau_real - out_real * tau_imag)
    total_real = jnp.sum(sum_real) / (4.0 * columns)
    total_imag = jnp.sum(sum_imag) / (4.0 * columns)
    row = lax.broadcasted_iota(jnp.int32, out_ref.shape, 0)
    column = lax.broadcasted_iota(jnp.int32, out_ref.shape, 1)
    total = jnp.where(row == 0, total_real, total_imag)
    out_ref[...] = jnp.where(column == pair, total, out_ref[...])


def elemental_kernel(where_ref, codes_ref, *refs):
    *halves, out_ref, table, rows_ref = refs
    fill(table, where_ref, [halves[i : i + 2] for i in range(0, len(halves), 2)])
    slices, slots, row_count = out_ref.shape[0], out_ref.shape[1], out_ref.shape[2]
    start = pl.multiple_of(where_ref[1] * row_count, row_count)
    for t in range(slices):
        for o in range(slots):
            real, imag = elemental(table, t ^ where_ref[0], codes_ref[o])
            rows_ref[0] = real
            rows_ref[1] = imag
            for part in range(2):
                out_ref[t, o, :, part] = rows_ref[part, pl.ds(start, row_count), :]


def shards(eigvecs, links, directions, pair_list, pair_operators, perambulators):
    slices, _, _, local_sites, columns = eigvecs.shape
    space = lax.axis_size("space")
    tm_size = lax.axis_size("tm")
    spin_size = lax.axis_size("spin")
    assert slices == spin_size and columns == LANES
    sites = PX * PY
    planes = local_sites // sites
    z_total = planes * space
    scale = 1.0 / math.sqrt(6.0 * sites * z_total)
    slots = directions.shape[0]
    pair_count, q_count = perambulators.shape[0], perambulators.shape[1]

    me = lax.axis_index("spin")
    where = jnp.stack(
        [me, lax.axis_index("space"), lax.axis_index("tm"), spin_size]
    ).astype(jnp.int32)
    lowest = lax.dynamic_slice(eigvecs, (me, 0, 0, 0, 0), (1, 2, 3, sites, columns))[0]
    halo = lax.ppermute(lowest, "space", [(i, (i - 1) % space) for i in range(space)])
    halo, other_codes = lax.optimization_barrier((halo, flip(directions, "spin", 1)))
    codes = jnp.concatenate([directions, other_codes])

    params = pltpu.CompilerParams(dimension_semantics=("arbitrary",), vmem_limit_bytes=50 << 20)
    stack_shape = pltpu.VMEM((3 * sites, 2 * LANES), jnp.bfloat16)
    f_shape = pltpu.VMEM((4 * LANES, 3 * sites), jnp.bfloat16)
    vt_shape = pltpu.VMEM((6, LANES, sites), jnp.float32)
    link_field = pltpu.with_memory_space_constraint(
        links.transpose(0, 1, 3, 4, 2, 5), pltpu.MemorySpace.HBM
    )
    estimate = lambda flops: pl.CostEstimate(flops=flops, bytes_accessed=1 << 22, transcendentals=0)
    half_rows = columns // 2
    part_a, inner = pl.pallas_call(
        partial(plane_kernel, scale=scale, step=2.0 * math.pi / z_total),
        out_shape=(
            jax.ShapeDtypeStruct((2, 4, half_rows, columns), jnp.float32),
            jax.ShapeDtypeStruct((columns, columns), jnp.float32),
        ),
        grid_spec=pltpu.PrefetchScalarGridSpec(
            num_scalar_prefetch=1,
            grid=(planes,),
            in_specs=[
                pl.BlockSpec((None, 2, 3, sites, columns), lambda z, w: (w[0], 0, 0, z, 0)),
                pl.BlockSpec((None, 2, 3, 3, 2, sites), lambda z, w: (w[0], 0, 0, 0, 0, z)),
                pl.BlockSpec(
                    (None, None, 3, 3, 2, sites),
                    lambda z, w: (w[0], 2, 0, 0, 0, jnp.maximum(z - 1, 0)),
                ),
            ],
            out_specs=(
                pl.BlockSpec((2, 4, half_rows, columns), lambda z, w: (0, 0, 0, 0)),
                pl.BlockSpec((columns, columns), lambda z, w: (0, 0)),
            ),
            scratch_shapes=[
                pltpu.VMEM((2, columns, columns), jnp.float32),
                vt_shape,
                pltpu.VMEM((2 * LANES, 3 * sites), jnp.bfloat16),
                stack_shape,
                stack_shape,
                stack_shape,
                stack_shape,
                pltpu.VMEM((3, 3, 3, 3, sites), jnp.float32),
                f_shape,
                f_shape,
                f_shape,
                pltpu.VMEM((3, 2 * LANES, 2 * LANES), jnp.float32),
            ],
        ),
        compiler_params=params,
        cost_estimate=estimate(20 * 10**9),
        name="planes",
    )(where, eigvecs, link_field, link_field)

    part_b = pl.pallas_call(
        partial(rim_kernel, scale=scale),
        out_shape=jax.ShapeDtypeStruct((2, 1, half_rows, columns), jnp.float32),
        grid_spec=pltpu.PrefetchScalarGridSpec(
            num_scalar_prefetch=1,
            grid=(1,),
            in_specs=[
                pl.BlockSpec((None, 2, 3, sites, columns), lambda z, w: (w[0], 0, 0, planes - 1, 0)),
                pl.BlockSpec((2, 3, sites, columns), lambda z, w: (0, 0, 0, 0)),
                pl.BlockSpec((None, None, 3, 3, 2, sites), lambda z, w: (w[0], 2, 0, 0, 0, planes - 1)),
                pl.BlockSpec((columns, columns), lambda z, w: (0, 0)),
            ],
            out_specs=pl.BlockSpec((2, 1, half_rows, columns), lambda z, w: (0, 0, 0, 0)),
            scratch_shapes=[
                vt_shape,
                stack_shape,
                pltpu.VMEM((3, 3, 3, sites), jnp.float32),
                f_shape,
            ],
        ),
        compiler_params=params,
        cost_estimate=estimate(2 * 10**9),
        name="rim",
    )(where, eigvecs, halo, link_field, inner)

    got_a = flip(part_a[1], "space", 1)
    got_b = flip(part_b[1], "space", 1)
    part_a, part_b = part_a[0], part_b[0]
    mask = 2
    while mask < space:
        part_a, got_a, part_b = lax.optimization_barrier((part_a, got_a, part_b))
        part_a, part_b = part_a + got_a, part_b + got_b
        got_a, got_b = flip(part_a, "space", mask), flip(part_b, "space", mask)
        mask *= 2

    mine = pl.pallas_call(
        round_kernel,
        out_shape=jax.ShapeDtypeStruct((5, half_rows, columns), jnp.bfloat16),
        compiler_params=pltpu.CompilerParams(vmem_limit_bytes=50 << 20),
        name="round",
    )(part_a, got_a, part_b, got_b)
    own = [mine, flip_both(mine, 1, 0)]
    for m in range(1, tm_size):
        own += [flip_both(mine, 0, m), flip_both(mine, 1, m)]
    other = [flip(half, "spin", 1) for half in own[:2]]

    whole = lambda shape: pl.BlockSpec(shape, lambda p, *_: (0,) * len(shape))

    row_count = columns // space
    elementals = pl.pallas_call(
        elemental_kernel,
        out_shape=jax.ShapeDtypeStruct((slices, slots, row_count, 2, columns), jnp.float32),
        grid_spec=pltpu.PrefetchScalarGridSpec(
            num_scalar_prefetch=2,
            grid=(1,),
            in_specs=[whole(mine.shape)] * 4,
            out_specs=whole((slices, slots, row_count, 2, columns)),
            scratch_shapes=[
                pltpu.VMEM((spin_size, 5, columns, columns), jnp.bfloat16),
                pltpu.VMEM((2, columns, columns), jnp.float32),
            ],
        ),
        compiler_params=params,
        name="rows",
    )(where, codes, *own[:2], *other)
    *rest, elementals = lax.optimization_barrier((*own[2:], elementals))
    own = own[:2] + rest
    other = other + [flip(half, "spin", 1) for half in rest]

    partial_corr = pl.pallas_call(
        partial(pair_kernel, tm_size=tm_size, slots=slots, q_count=q_count),
        out_shape=jax.ShapeDtypeStruct((2, pair_count), jnp.float32),
        grid_spec=pltpu.PrefetchScalarGridSpec(
            num_scalar_prefetch=4,
            grid=(pair_count,),
            in_specs=[whole(mine.shape)] * (2 * len(own))
            + [
                pl.BlockSpec((None, q_count, 2, columns, columns), lambda p, *_: (p, 0, 0, 0, 0)),
            ],
            out_specs=whole((2, pair_count)),
            scratch_shapes=[
                pltpu.VMEM((spin_size * tm_size, 5, columns, columns), jnp.bfloat16)
            ],
        ),
        compiler_params=params,
        name="pairs",
    )(where, codes, pair_list.T, pair_operators.T, *own, *other, perambulators)
    correlators = (partial_corr + flip(partial_corr, "spin", 1)).T

    return elementals, correlators


def solution(mesh):
    return jax.shard_map(
        shards,
        mesh=mesh,
        in_specs=(
            P("tm", None, None, "space", None),
            P("tm", None, None, None, None, "space"),
            P("spin"),
            P(("space", "tm"), None),
            P(("space", "tm"), None),
            P(("space", "tm"), "spin", None, None, None),
        ),
        out_specs=(P(("ens", "tm"), "spin", "space", None, None), P(("ens", "space", "tm"), None)),
        check_vma=False,
    )
```

```python
from functools import partial
import math

import jax
import jax.numpy as jnp
from jax import lax
from jax.experimental import pallas as pl
from jax.experimental.pallas import tpu as pltpu
from jax.sharding import PartitionSpec as P

PX = 16
PY = 16
LANES = 128
ROWS = 16


def flip(array, axis, mask):
    count = lax.axis_size(axis)
    return lax.ppermute(array, axis, [(i, i ^ mask) for i in range(count)])


def flip_both(array, space_mask, tm_mask):
    space, tm = lax.axis_size("space"), lax.axis_size("tm")
    pairs = [
        (z * tm + x, (z ^ space_mask) * tm + (x ^ tm_mask)) for z in range(space) for x in range(tm)
    ]
    return lax.ppermute(array, ("space", "tm"), pairs)


def transposed_plane(v_ref, vt_ref):
    for part in range(2):
        for colour in range(3):
            vt_ref[3 * part + colour] = v_ref[part, colour].astype(jnp.float32).T


def stacked_plane(v_ref, vr_ref, shift=0):
    sites = v_ref.shape[2]
    for part in range(2):
        columns = slice(part * LANES, (part + 1) * LANES)
        for colour in range(3):
            start = colour * sites
            if shift:
                vr_ref[start : start + shift, columns] = v_ref[part, colour, sites - shift :]
            vr_ref[start + shift : start + sites, columns] = v_ref[part, colour, : sites - shift]


def permuted_plane(v_ref, vr_ref, permutation):
    sites = v_ref.shape[2]
    for colour in range(3):
        plane = jnp.concatenate([v_ref[0, colour], v_ref[1, colour]], 1)
        vr_ref[colour * sites : (colour + 1) * sites] = dot(permutation, plane).astype(jnp.bfloat16)


def link_sums(u, uf_ref):
    real, imag = u[..., 0:1, :], u[..., 1:2, :]
    uf_ref[..., 0:1, :] = real
    uf_ref[..., 1:2, :] = imag - real
    uf_ref[..., 2:3, :] = imag + real


def turned(u, amount):
    sites = u.shape[-1]
    return jnp.concatenate([u[..., sites - amount :], u[..., : sites - amount]], -1)


def link_rows(uf_ref, lead, lanes):
    return [
        [[uf_ref[lead + (a, b, slice(i, i + 1), lanes)] for b in range(3)] for a in range(3)]
        for i in range(3)
    ]


def times_links(rows, vectors, f_ref, k_tile, lanes, sites):
    sums = [vectors[0][b] + vectors[1][b] for b in range(3)]
    for a in range(3):
        k1 = sum_products(rows[0][a], sums)
        k2 = sum_products(rows[1][a], vectors[0])
        k3 = sum_products(rows[2][a], vectors[1])
        for part, value in ((0, k1 - k3), (1, k1 + k2)):
            start = part * LANES + k_tile * ROWS
            high = value.astype(jnp.bfloat16)
            low = (value - high.astype(jnp.float32)).astype(jnp.bfloat16)
            columns = slice(a * sites + lanes.start, a * sites + lanes.stop)
            for copy, piece in ((0, high), (1, low)):
                at = copy * 2 * LANES + start
                f_ref[at : at + ROWS, columns] = piece


def direction(rows_of, vt, f_ref):
    sites = vt.shape[2]
    for j in range(sites // LANES):
        lanes = slice(j * LANES, (j + 1) * LANES)
        rows = rows_of(lanes)
        for k_tile in range(LANES // ROWS):
            k = slice(k_tile * ROWS, (k_tile + 1) * ROWS)
            vectors = [[vt[3 * part + c, k, lanes] for c in range(3)] for part in range(2)]
            times_links(rows, vectors, f_ref, k_tile, lanes, sites)


def gram(f_ref, vr_ref):
    both = dot(f_ref[...], vr_ref[...])
    return both[: 2 * LANES] + both[2 * LANES :]


def sum_products(left, right):
    return left[0] * right[0] + left[1] * right[1] + left[2] * right[2]


def block(acc, q, p):
    return acc[q * LANES : (q + 1) * LANES, p * LANES : (p + 1) * LANES]


def upper(shape):
    row = lax.broadcasted_iota(jnp.int32, shape, 0)
    column = lax.broadcasted_iota(jnp.int32, shape, 1)
    return row <= column


def antihermitian(acc, scale):
    real = block(acc, 0, 0) + block(acc, 1, 1)
    imag = block(acc, 1, 0) - block(acc, 0, 1)
    e_real = scale * (real.T - real)
    e_imag = scale * (imag.T + imag)
    return jnp.where(upper(real.shape), e_imag, e_real)


def dot(left, right):
    return jnp.dot(left, right, preferred_element_type=jnp.float32)


def store_halves(out_ref, at, matrix, parity):
    half_rows = matrix.shape[0] // 2
    for half in range(2):
        out_ref[parity ^ half, at] = matrix[half * half_rows : (half + 1) * half_rows]


def plane_kernel(
    where_ref, v_ref, u_ref, below_ref, out_ref, inner_ref,
    waves, turn, vt, vtb, vr, vx, vy, uf, f0, f1, f2, acc, *, scale, step
):
    pair = pl.program_id(0)
    pairs = pl.num_programs(0)
    sites = turn.shape[0]

    @pl.when(pair == 0)
    def _():
        acc[...] = jnp.zeros_like(acc)
        waves[...] = jnp.zeros_like(waves)
        vr[...] = jnp.zeros_like(vr)
        f2[1] = jnp.zeros_like(f2[1])
        column = lax.broadcasted_iota(jnp.int32, turn.shape, 1)
        row = lax.broadcasted_iota(jnp.int32, turn.shape, 0)
        before = row - row % PX + (row + PX - 1) % PX
        turn[...] = jnp.where(column == before, 1.0, 0.0).astype(jnp.bfloat16)

    acc[2] += gram(f2.at[1], vr.at[0])
    for i in range(2):
        here = slice(i * sites, (i + 1) * sites)
        v_here = v_ref.at[:, :, here]
        transposed_plane(v_here, vt.at[i])
        stacked_plane(v_here, vr.at[i])
        stacked_plane(v_here, vy.at[i], PX)
        permuted_plane(v_here, vx.at[i], turn[...])

        u0 = u_ref[0, :, :, :, here].astype(jnp.float32)
        lane = lax.broadcasted_iota(jnp.int32, u0.shape, 3)
        link_sums(jnp.where(lane % PX == 0, turned(u0, sites - PX + 1), turned(u0, 1)), uf.at[i, 0])
        link_sums(turned(u_ref[1, :, :, :, here].astype(jnp.float32), PX), uf.at[i, 1])
        below = below_ref[...] if i == 0 else u_ref[2, :, :, :, :sites]
        link_sums(below.astype(jnp.float32), uf.at[i, 2])

        direction(partial(link_rows, uf.at[i], (0,)), vt.at[i], f0.at[i])
        for part in range(2):
            for colour in range(3):
                vtb[i, part * LANES : (part + 1) * LANES, colour * sites : (colour + 1) * sites] = vt[
                    i, 3 * part + colour
                ].astype(jnp.bfloat16)
        own = dot(vtb[i], vr[i])
        g_real = block(own, 0, 0) + block(own, 1, 1)
        g_imag = block(own, 0, 1) - block(own, 1, 0)
        packed = jnp.where(upper(g_real.shape), g_real, g_imag)
        z = (where_ref[1] * pairs + pair) * 2 + i
        angle = step * jnp.full((8, LANES), z, jnp.int32).astype(jnp.float32)
        waves[0] += jnp.cos(angle)[0:1] * packed
        waves[1] += jnp.sin(angle)[0:1] * packed

        acc[0] += gram(f0.at[i], vx.at[i])
        direction(partial(link_rows, uf.at[i], (1,)), vt.at[i], f1.at[i])
        acc[1] += gram(f1.at[i], vy.at[i])
        direction(partial(link_rows, uf.at[i], (2,)), vt.at[i], f2.at[i])
        if i == 0:
            acc[2] += gram(f2.at[0], vr.at[1])

    @pl.when(pair == pairs - 1)
    def _():
        parity = where_ref[1] % 2
        cos_sym, cos_anti = unpack(scale * waves[0])
        sin_sym, sin_anti = unpack(scale * waves[1])
        store_halves(out_ref, 0, antihermitian(acc[0], 0.5 * scale), parity)
        store_halves(out_ref, 1, antihermitian(acc[1], 0.5 * scale), parity)
        store_halves(out_ref, 2, cos_sym + sin_anti, parity)
        store_halves(out_ref, 3, cos_anti - sin_sym, parity)
        inner_ref[...] = antihermitian(acc[2] + gram(f2.at[1], vr.at[0]), 0.5 * scale)


def rim_kernel(where_ref, v_ref, halo_ref, u_ref, inner_ref, out_ref, vt, vr, uf, f2, *, scale):
    link_sums(u_ref[...].astype(jnp.float32), uf)
    transposed_plane(halo_ref, vt)
    stacked_plane(v_ref, vr)
    direction(partial(link_rows, uf, ()), vt, f2)
    total = inner_ref[...] + antihermitian(gram(f2, vr), 0.5 * scale)
    store_halves(out_ref, 0, total, where_ref[1] % 2)


def unpack(packed):
    flipped = packed.T
    row = lax.broadcasted_iota(jnp.int32, packed.shape, 0)
    column = lax.broadcasted_iota(jnp.int32, packed.shape, 1)
    symmetric = jnp.where(row <= column, packed, flipped)
    antisymmetric = jnp.where(row > column, packed, jnp.where(row < column, -flipped, 0.0))
    return symmetric, antisymmetric


def round_kernel(mine_a, got_a, mine_b, got_b, out_ref):
    sums = mine_a[...] + got_a[...]
    out_ref[0] = sums[0].astype(jnp.bfloat16)
    out_ref[1] = sums[1].astype(jnp.bfloat16)
    out_ref[2] = (mine_b[0] + got_b[0]).astype(jnp.bfloat16)
    out_ref[3] = sums[2].astype(jnp.bfloat16)
    out_ref[4] = sums[3].astype(jnp.bfloat16)


def elemental(table, slot, code):
    third = code == 3
    packed = table[slot, jnp.where(third, 3, code)].astype(jnp.float32)
    other = table[slot, 4].astype(jnp.float32)
    symmetric, antisymmetric = unpack(packed)
    real = jnp.where(third, packed, antisymmetric)
    imag = jnp.where(third, other, symmetric)
    return real, imag


def fill(table, where_ref, parts):
    half_rows = table.shape[2] // 2
    parity = where_ref[1] % 2
    for at, halves in enumerate(parts):
        for i, half in enumerate(halves):
            start = pl.multiple_of((parity ^ i) * half_rows, half_rows)
            table[at, :, pl.ds(start, half_rows), :] = half[...]


def slot_of(where_ref, slice_index, tm_size):
    spin_size = where_ref[3]
    owner = slice_index // spin_size
    within = slice_index % spin_size
    return (within ^ where_ref[0]) * tm_size + (owner ^ where_ref[2])


def folded(values):
    return jnp.sum(values.reshape(-1, 8, values.shape[1]), axis=0)


def pair_kernel(where_ref, codes_ref, pairs_ref, operators_ref, *refs, tm_size, slots):
    *halves, tau_ref, out_ref, table, h_ref, second_ref = refs
    pair_count, q_count = tau_ref.shape[0], tau_ref.shape[1]
    columns = LANES
    fill(table, where_ref, [halves[i : i + 2] for i in range(0, len(halves), 2)])

    def matrix(pair, end):
        operator = operators_ref[end, pair]
        core = operator // slots
        code = codes_ref[(core ^ where_ref[0]) * slots + operator % slots]
        slot = slot_of(where_ref, pairs_ref[end, pair], tm_size)
        real, imag = elemental(table, slot, code)
        return real.astype(jnp.bfloat16), imag.astype(jnp.bfloat16)

    row = lax.broadcasted_iota(jnp.int32, out_ref.shape, 0)
    column = lax.broadcasted_iota(jnp.int32, out_ref.shape, 1)
    result = jnp.zeros(out_ref.shape, jnp.float32)
    for pair in range(pair_count):
        at = pair % 2
        r_real, r_imag = matrix(pair, 0)
        s_real, s_imag = matrix(pair, 1)
        sink = jnp.concatenate(
            [
                jnp.concatenate([s_real, -s_imag], 1),
                jnp.concatenate([s_imag, s_real], 1),
            ],
            0,
        )
        source = jnp.concatenate(
            [
                jnp.concatenate([r_real, r_imag], 1),
                jnp.concatenate([-r_imag, r_real], 1),
            ],
            0,
        )
        twice = jnp.concatenate([source, source], 0)
        for q in range(0, q_count, 2):
            pairwise = jnp.concatenate(
                [tau_ref[pair, q + i].reshape(2 * columns, columns) for i in range(2)], 1
            )
            halfway = dot(sink, pairwise)
            for i in range(2):
                rows = slice((q + i) * columns, (q + i + 1) * columns)
                for part in range(2):
                    value = halfway[
                        part * columns : (part + 1) * columns, i * columns : (i + 1) * columns
                    ]
                    high = value.astype(jnp.bfloat16)
                    low = (value - high.astype(jnp.float32)).astype(jnp.bfloat16)
                    h_ref[at, rows, part * columns : (part + 1) * columns] = high
                    h_ref[at, rows, (2 + part) * columns : (3 + part) * columns] = low
        for q in range(0, q_count, 4):
            rows = slice(q * columns, (q + 4) * columns)
            second_ref[at, rows] = dot(h_ref[at, rows], twice)
        sum_real = jnp.zeros((8, columns), jnp.float32)
        sum_imag = jnp.zeros((8, columns), jnp.float32)
        for q in range(q_count):
            spin_pair = where_ref[0] * q_count + q
            sign = jnp.where((spin_pair // 4 < 2) == (spin_pair % 4 < 2), 1.0, -1.0)
            part_real = jnp.zeros((8, columns), jnp.float32)
            part_imag = jnp.zeros((8, columns), jnp.float32)
            for start in range(0, columns, 16):
                rows = slice(q * columns + start, q * columns + start + 16)
                out_real = second_ref[at, rows, :columns]
                out_imag = second_ref[at, rows, columns:]
                tau_real = tau_ref[pair, q, 0, start : start + 16].astype(jnp.float32)
                tau_imag = tau_ref[pair, q, 1, start : start + 16].astype(jnp.float32)
                part_real += folded(out_real * tau_real + out_imag * tau_imag)
                part_imag += folded(out_imag * tau_real - out_real * tau_imag)
            sum_real += sign * part_real
            sum_imag += sign * part_imag
        total_real = jnp.sum(sum_real) / (4.0 * columns)
        total_imag = jnp.sum(sum_imag) / (4.0 * columns)
        result = jnp.where(column == pair, jnp.where(row == 0, total_real, total_imag), result)
    out_ref[...] = result


def elemental_kernel(where_ref, codes_ref, *refs):
    *halves, out_ref, table, rows_ref = refs
    fill(table, where_ref, [halves[i : i + 2] for i in range(0, len(halves), 2)])
    slices, slots, row_count = out_ref.shape[0], out_ref.shape[1], out_ref.shape[2]
    start = pl.multiple_of(where_ref[1] * row_count, row_count)
    for t in range(slices):
        for o in range(slots):
            real, imag = elemental(table, t ^ where_ref[0], codes_ref[o])
            rows_ref[0] = real
            rows_ref[1] = imag
            for part in range(2):
                out_ref[t, o, :, part] = rows_ref[part, pl.ds(start, row_count), :]


def shards(eigvecs, links, directions, pair_list, pair_operators, perambulators):
    slices, _, _, local_sites, columns = eigvecs.shape
    space = lax.axis_size("space")
    tm_size = lax.axis_size("tm")
    spin_size = lax.axis_size("spin")
    assert slices == spin_size and columns == LANES
    assert local_sites % (2 * PX * PY) == 0
    sites = PX * PY
    planes = local_sites // sites
    z_total = planes * space
    scale = 1.0 / math.sqrt(6.0 * sites * z_total)
    slots = directions.shape[0]
    pair_count, q_count = perambulators.shape[0], perambulators.shape[1]

    me = lax.axis_index("spin")
    where = jnp.stack(
        [me, lax.axis_index("space"), lax.axis_index("tm"), spin_size]
    ).astype(jnp.int32)
    lowest = lax.dynamic_slice(eigvecs, (me, 0, 0, 0, 0), (1, 2, 3, sites, columns))[0]
    halo = lax.ppermute(lowest, "space", [(i, (i - 1) % space) for i in range(space)])
    halo, other_codes = lax.optimization_barrier((halo, flip(directions, "spin", 1)))
    codes = jnp.concatenate([directions, other_codes])

    params = pltpu.CompilerParams(dimension_semantics=("arbitrary",), vmem_limit_bytes=50 << 20)
    stack_shape = pltpu.VMEM((3 * sites, 2 * LANES), jnp.bfloat16)
    f_shape = pltpu.VMEM((4 * LANES, 3 * sites), jnp.bfloat16)
    vt_shape = pltpu.VMEM((6, LANES, sites), jnp.float32)
    link_field = pltpu.with_memory_space_constraint(
        links.transpose(0, 1, 3, 4, 2, 5), pltpu.MemorySpace.HBM
    )
    estimate = lambda flops: pl.CostEstimate(flops=flops, bytes_accessed=1 << 22, transcendentals=0)
    half_rows = columns // 2
    part_a, inner = pl.pallas_call(
        partial(plane_kernel, scale=scale, step=2.0 * math.pi / z_total),
        out_shape=(
            jax.ShapeDtypeStruct((2, 4, half_rows, columns), jnp.float32),
            jax.ShapeDtypeStruct((columns, columns), jnp.float32),
        ),
        grid_spec=pltpu.PrefetchScalarGridSpec(
            num_scalar_prefetch=1,
            grid=(planes // 2,),
            in_specs=[
                pl.BlockSpec((None, 2, 3, 2 * sites, columns), lambda z, w: (w[0], 0, 0, z, 0)),
                pl.BlockSpec((None, 3, 3, 3, 2, 2 * sites), lambda z, w: (w[0], 0, 0, 0, 0, z)),
                pl.BlockSpec(
                    (None, None, 3, 3, 2, sites),
                    lambda z, w: (w[0], 2, 0, 0, 0, jnp.maximum(2 * z - 1, 0)),
                ),
            ],
            out_specs=(
                pl.BlockSpec((2, 4, half_rows, columns), lambda z, w: (0, 0, 0, 0)),
                pl.BlockSpec((columns, columns), lambda z, w: (0, 0)),
            ),
            scratch_shapes=[
                pltpu.VMEM((2, columns, columns), jnp.float32),
                pltpu.VMEM((sites, sites), jnp.bfloat16),
                pltpu.VMEM((2, 6, LANES, sites), jnp.float32),
                pltpu.VMEM((2, 2 * LANES, 3 * sites), jnp.bfloat16),
                pltpu.VMEM((2, 3 * sites, 2 * LANES), jnp.bfloat16),
                pltpu.VMEM((2, 3 * sites, 2 * LANES), jnp.bfloat16),
                pltpu.VMEM((2, 3 * sites, 2 * LANES), jnp.bfloat16),
                pltpu.VMEM((2, 3, 3, 3, 3, sites), jnp.float32),
                pltpu.VMEM((2, 4 * LANES, 3 * sites), jnp.bfloat16),
                pltpu.VMEM((2, 4 * LANES, 3 * sites), jnp.bfloat16),
                pltpu.VMEM((2, 4 * LANES, 3 * sites), jnp.bfloat16),
                pltpu.VMEM((3, 2 * LANES, 2 * LANES), jnp.float32),
            ],
        ),
        compiler_params=pltpu.CompilerParams(
            dimension_semantics=("arbitrary",),
            vmem_limit_bytes=50 << 20,
        ),
        cost_estimate=estimate(20 * 10**9),
        name="planes",
    )(where, eigvecs, link_field, link_field)

    part_b = pl.pallas_call(
        partial(rim_kernel, scale=scale),
        out_shape=jax.ShapeDtypeStruct((2, 1, half_rows, columns), jnp.float32),
        grid_spec=pltpu.PrefetchScalarGridSpec(
            num_scalar_prefetch=1,
            grid=(1,),
            in_specs=[
                pl.BlockSpec((None, 2, 3, sites, columns), lambda z, w: (w[0], 0, 0, planes - 1, 0)),
                pl.BlockSpec(memory_space=pltpu.VMEM),
                pl.BlockSpec((None, None, 3, 3, 2, sites), lambda z, w: (w[0], 2, 0, 0, 0, planes - 1)),
                pl.BlockSpec(memory_space=pltpu.VMEM),
            ],
            out_specs=pl.BlockSpec((2, 1, half_rows, columns), lambda z, w: (0, 0, 0, 0)),
            scratch_shapes=[
                vt_shape,
                stack_shape,
                pltpu.VMEM((3, 3, 3, sites), jnp.float32),
                f_shape,
            ],
        ),
        compiler_params=params,
        cost_estimate=estimate(2 * 10**9),
        name="rim",
    )(where, eigvecs, halo, link_field, inner)

    got_a = flip(part_a[1], "space", 1)
    got_b = flip(part_b[1], "space", 1)
    part_a, part_b = part_a[0], part_b[0]
    mask = 2
    while mask < space:
        part_a, got_a, part_b = lax.optimization_barrier((part_a, got_a, part_b))
        part_a, part_b = part_a + got_a, part_b + got_b
        got_a, got_b = flip(part_a, "space", mask), flip(part_b, "space", mask)
        mask *= 2

    mine = pl.pallas_call(
        round_kernel,
        out_shape=jax.ShapeDtypeStruct((5, half_rows, columns), jnp.bfloat16),
        compiler_params=pltpu.CompilerParams(vmem_limit_bytes=50 << 20),
        name="round",
    )(part_a, got_a, part_b, got_b)
    own = [mine, flip_both(mine, 1, 0)]
    for m in range(1, tm_size):
        own += [flip_both(mine, 0, m), flip_both(mine, 1, m)]
    other = [flip(half, "spin", 1) for half in own[:2]]

    resident = pl.BlockSpec(memory_space=pltpu.VMEM)
    whole = lambda shape: pl.BlockSpec(shape, lambda p, *_: (0,) * len(shape))

    row_count = columns // space
    elementals = pl.pallas_call(
        elemental_kernel,
        out_shape=jax.ShapeDtypeStruct((slices, slots, row_count, 2, columns), jnp.float32),
        grid_spec=pltpu.PrefetchScalarGridSpec(
            num_scalar_prefetch=2,
            grid=(1,),
            in_specs=[resident] * 4,
            out_specs=whole((slices, slots, row_count, 2, columns)),
            scratch_shapes=[
                pltpu.VMEM((spin_size, 5, columns, columns), jnp.bfloat16),
                pltpu.VMEM((2, columns, columns), jnp.float32),
            ],
        ),
        compiler_params=params,
        name="rows",
    )(where, codes, *own[:2], *other)
    *rest, elementals = lax.optimization_barrier((*own[2:], elementals))
    own = own[:2] + rest
    other = other + [flip(half, "spin", 1) for half in rest]

    partial_corr = pl.pallas_call(
        partial(pair_kernel, tm_size=tm_size, slots=slots),
        out_shape=jax.ShapeDtypeStruct((2, pair_count), jnp.float32),
        grid_spec=pltpu.PrefetchScalarGridSpec(
            num_scalar_prefetch=4,
            grid=(1,),
            in_specs=[resident] * (2 * len(own) + 1),
            out_specs=whole((2, pair_count)),
            scratch_shapes=[
                pltpu.VMEM((spin_size * tm_size, 5, columns, columns), jnp.bfloat16),
                pltpu.VMEM((2, q_count * columns, 4 * columns), jnp.bfloat16),
                pltpu.VMEM((2, q_count * columns, 2 * columns), jnp.float32),
            ],
        ),
        compiler_params=params,
        name="pairs",
    )(where, codes, pair_list.T, pair_operators.T, *own, *other, perambulators)
    correlators = (partial_corr + flip(partial_corr, "spin", 1)).T

    return elementals, correlators


def solution(mesh):
    return jax.shard_map(
        shards,
        mesh=mesh,
        in_specs=(
            P("tm", None, None, "space", None),
            P("tm", None, None, None, None, "space"),
            P("spin"),
            P(("space", "tm"), None),
            P(("space", "tm"), None),
            P(("space", "tm"), "spin", None, None, None),
        ),
        out_specs=(P(("ens", "tm"), "spin", "space", None, None), P(("ens", "space", "tm"), None)),
        check_vma=False,
    )
```

```python
from functools import partial
import math

import jax
import jax.numpy as jnp
from jax import lax
from jax.experimental import pallas as pl
from jax.experimental.pallas import tpu as pltpu
from jax.sharding import PartitionSpec as P

PX = 16
PY = 16
LANES = 128
ROWS = 16


def flip(array, axis, mask):
    count = lax.axis_size(axis)
    return lax.ppermute(array, axis, [(i, i ^ mask) for i in range(count)])


def flip_by_core(array, space_masks, tm_mask=0):
    space, tm, spin = lax.axis_size("space"), lax.axis_size("tm"), lax.axis_size("spin")
    pairs = [
        ((z * tm + x) * spin + c, ((z ^ space_masks[c]) * tm + (x ^ tm_mask)) * spin + c)
        for z in range(space)
        for x in range(tm)
        for c in range(spin)
    ]
    return lax.ppermute(array, ("space", "tm", "spin"), pairs)


def transposed_plane(v_ref, vt_ref):
    for part in range(2):
        for colour in range(3):
            vt_ref[3 * part + colour] = v_ref[part, colour].astype(jnp.float32).T


def stacked_plane(v_ref, vr_ref, shift=0):
    sites = v_ref.shape[2]
    for part in range(2):
        columns = slice(part * LANES, (part + 1) * LANES)
        for colour in range(3):
            start = colour * sites
            if shift:
                vr_ref[start : start + shift, columns] = v_ref[part, colour, sites - shift :]
            vr_ref[start + shift : start + sites, columns] = v_ref[part, colour, : sites - shift]


def permuted_plane(v_ref, vr_ref, permutation):
    sites = v_ref.shape[2]
    for colour in range(3):
        plane = jnp.concatenate([v_ref[0, colour], v_ref[1, colour]], 1)
        vr_ref[colour * sites : (colour + 1) * sites] = dot(permutation, plane).astype(jnp.bfloat16)


def link_sums(u, uf_ref):
    real, imag = u[..., 0:1, :], u[..., 1:2, :]
    uf_ref[..., 0:1, :] = real
    uf_ref[..., 1:2, :] = imag - real
    uf_ref[..., 2:3, :] = imag + real


def turned(u, amount):
    sites = u.shape[-1]
    return jnp.concatenate([u[..., sites - amount :], u[..., : sites - amount]], -1)


def link_rows(uf_ref, lead, lanes):
    return [
        [[uf_ref[lead + (a, b, slice(i, i + 1), lanes)] for b in range(3)] for a in range(3)]
        for i in range(3)
    ]


def times_links(rows, vectors, f_ref, k_tile, lanes, sites):
    sums = [vectors[0][b] + vectors[1][b] for b in range(3)]
    for a in range(3):
        k1 = sum_products(rows[0][a], sums)
        k2 = sum_products(rows[1][a], vectors[0])
        k3 = sum_products(rows[2][a], vectors[1])
        for part, value in ((0, k1 - k3), (1, k1 + k2)):
            start = part * LANES + k_tile * ROWS
            high = value.astype(jnp.bfloat16)
            low = (value - high.astype(jnp.float32)).astype(jnp.bfloat16)
            columns = slice(a * sites + lanes.start, a * sites + lanes.stop)
            for copy, piece in ((0, high), (1, low)):
                at = copy * 2 * LANES + start
                f_ref[at : at + ROWS, columns] = piece


def direction(rows_of, vt, f_ref):
    sites = vt.shape[2]
    for j in range(sites // LANES):
        lanes = slice(j * LANES, (j + 1) * LANES)
        rows = rows_of(lanes)
        for k_tile in range(LANES // ROWS):
            k = slice(k_tile * ROWS, (k_tile + 1) * ROWS)
            vectors = [[vt[3 * part + c, k, lanes] for c in range(3)] for part in range(2)]
            times_links(rows, vectors, f_ref, k_tile, lanes, sites)


def gram(f_ref, vr_ref):
    both = dot(f_ref[...], vr_ref[...])
    return both[: 2 * LANES] + both[2 * LANES :]


def sum_products(left, right):
    return left[0] * right[0] + left[1] * right[1] + left[2] * right[2]


def block(acc, q, p):
    return acc[q * LANES : (q + 1) * LANES, p * LANES : (p + 1) * LANES]


def upper(shape):
    row = lax.broadcasted_iota(jnp.int32, shape, 0)
    column = lax.broadcasted_iota(jnp.int32, shape, 1)
    return row <= column


def antihermitian(acc, scale):
    real = block(acc, 0, 0) + block(acc, 1, 1)
    imag = block(acc, 1, 0) - block(acc, 0, 1)
    e_real = scale * (real.T - real)
    e_imag = scale * (imag.T + imag)
    return jnp.where(upper(real.shape), e_imag, e_real)


def dot(left, right):
    return jnp.dot(left, right, preferred_element_type=jnp.float32)


def store_halves(out_ref, at, matrix, parity):
    half_rows = matrix.shape[0] // 2
    for half in range(2):
        out_ref[parity ^ half, at] = matrix[half * half_rows : (half + 1) * half_rows]


def plane_kernel(
    where_ref, v_ref, u_ref, below_ref, out_ref, inner_ref,
    waves, turn, vt, vtb, vr, vx, vy, uf, f0, f1, f2, acc, *, scale, step
):
    pair = pl.program_id(0)
    pairs = pl.num_programs(0)
    sites = turn.shape[0]

    @pl.when(pair == 0)
    def _():
        acc[...] = jnp.zeros_like(acc)
        waves[...] = jnp.zeros_like(waves)
        vr[...] = jnp.zeros_like(vr)
        f2[1] = jnp.zeros_like(f2[1])
        column = lax.broadcasted_iota(jnp.int32, turn.shape, 1)
        row = lax.broadcasted_iota(jnp.int32, turn.shape, 0)
        before = row - row % PX + (row + PX - 1) % PX
        turn[...] = jnp.where(column == before, 1.0, 0.0).astype(jnp.bfloat16)

    acc[2] += gram(f2.at[1], vr.at[0])
    for i in range(2):
        here = slice(i * sites, (i + 1) * sites)
        v_here = v_ref.at[:, :, here]
        transposed_plane(v_here, vt.at[i])
        stacked_plane(v_here, vr.at[i])
        stacked_plane(v_here, vy.at[i], PX)
        permuted_plane(v_here, vx.at[i], turn[...])

        u0 = u_ref[0, :, :, :, here].astype(jnp.float32)
        lane = lax.broadcasted_iota(jnp.int32, u0.shape, 3)
        link_sums(jnp.where(lane % PX == 0, turned(u0, sites - PX + 1), turned(u0, 1)), uf.at[i, 0])
        link_sums(turned(u_ref[1, :, :, :, here].astype(jnp.float32), PX), uf.at[i, 1])
        below = below_ref[...] if i == 0 else u_ref[2, :, :, :, :sites]
        link_sums(below.astype(jnp.float32), uf.at[i, 2])

        direction(partial(link_rows, uf.at[i], (0,)), vt.at[i], f0.at[i])
        for part in range(2):
            for colour in range(3):
                vtb[i, part * LANES : (part + 1) * LANES, colour * sites : (colour + 1) * sites] = vt[
                    i, 3 * part + colour
                ].astype(jnp.bfloat16)
        own = dot(vtb[i], vr[i])
        g_real = block(own, 0, 0) + block(own, 1, 1)
        g_imag = block(own, 0, 1) - block(own, 1, 0)
        packed = jnp.where(upper(g_real.shape), g_real, g_imag)
        z = (where_ref[1] * pairs + pair) * 2 + i
        angle = step * jnp.full((8, LANES), z, jnp.int32).astype(jnp.float32)
        waves[0] += jnp.cos(angle)[0:1] * packed
        waves[1] += jnp.sin(angle)[0:1] * packed

        acc[0] += gram(f0.at[i], vx.at[i])
        direction(partial(link_rows, uf.at[i], (1,)), vt.at[i], f1.at[i])
        acc[1] += gram(f1.at[i], vy.at[i])
        direction(partial(link_rows, uf.at[i], (2,)), vt.at[i], f2.at[i])
        if i == 0:
            acc[2] += gram(f2.at[0], vr.at[1])

    @pl.when(pair == pairs - 1)
    def _():
        parity = where_ref[4]
        cos_sym, cos_anti = unpack(scale * waves[0])
        sin_sym, sin_anti = unpack(scale * waves[1])
        store_halves(out_ref, 0, antihermitian(acc[0], 0.5 * scale), parity)
        store_halves(out_ref, 1, antihermitian(acc[1], 0.5 * scale), parity)
        store_halves(out_ref, 2, cos_sym + sin_anti, parity)
        store_halves(out_ref, 3, cos_anti - sin_sym, parity)
        inner_ref[...] = antihermitian(acc[2] + gram(f2.at[1], vr.at[0]), 0.5 * scale)


def rim_kernel(where_ref, v_ref, halo_ref, u_ref, inner_ref, out_ref, vt, vr, uf, f2, *, scale):
    link_sums(u_ref[...].astype(jnp.float32), uf)
    transposed_plane(halo_ref, vt)
    stacked_plane(v_ref, vr)
    direction(partial(link_rows, uf, ()), vt, f2)
    total = inner_ref[...] + antihermitian(gram(f2, vr), 0.5 * scale)
    store_halves(out_ref, 0, total, where_ref[4])


def unpack(packed):
    flipped = packed.T
    row = lax.broadcasted_iota(jnp.int32, packed.shape, 0)
    column = lax.broadcasted_iota(jnp.int32, packed.shape, 1)
    symmetric = jnp.where(row <= column, packed, flipped)
    antisymmetric = jnp.where(row > column, packed, jnp.where(row < column, -flipped, 0.0))
    return symmetric, antisymmetric


def join_kernel(part_a, got_a, part_b, got_b, out_ref):
    out_ref[:4] = part_a[0] + got_a[...]
    out_ref[4] = part_b[0, 0] + got_b[0]


def round_kernel(mine, got, out_ref):
    sums = mine[...] + got[...]
    for at, source in enumerate((0, 1, 4, 2, 3)):
        out_ref[at] = sums[source].astype(jnp.bfloat16)


def elemental(table, slot, code):
    third = code == 3
    packed = table[slot, jnp.where(third, 3, code)].astype(jnp.float32)
    other = table[slot, 4].astype(jnp.float32)
    symmetric, antisymmetric = unpack(packed)
    real = jnp.where(third, packed, antisymmetric)
    imag = jnp.where(third, other, symmetric)
    return real, imag


def fill(table, where_ref, parts):
    half_rows = table.shape[2] // 2
    for at, halves in enumerate(parts):
        parity = where_ref[4] if at < len(parts) // 2 else where_ref[5]
        for i, half in enumerate(halves):
            start = pl.multiple_of((parity ^ i) * half_rows, half_rows)
            table[at, :, pl.ds(start, half_rows), :] = half[...]


def slot_of(where_ref, slice_index, tm_size):
    spin_size = where_ref[3]
    owner = slice_index // spin_size
    within = slice_index % spin_size
    return (within ^ where_ref[0]) * tm_size + (owner ^ where_ref[2])


def folded(values):
    return jnp.sum(values.reshape(-1, 8, values.shape[1]), axis=0)


def pair_kernel(where_ref, codes_ref, pairs_ref, operators_ref, *refs, tm_size, slots):
    *halves, tau_ref, out_ref, table, h_ref, second_ref = refs
    pair_count, q_count = tau_ref.shape[0], tau_ref.shape[1]
    columns = LANES
    fill(table, where_ref, [halves[i : i + 2] for i in range(0, len(halves), 2)])

    def matrix(pair, end):
        operator = operators_ref[end, pair]
        core = operator // slots
        code = codes_ref[(core ^ where_ref[0]) * slots + operator % slots]
        slot = slot_of(where_ref, pairs_ref[end, pair], tm_size)
        real, imag = elemental(table, slot, code)
        return real.astype(jnp.bfloat16), imag.astype(jnp.bfloat16)

    row = lax.broadcasted_iota(jnp.int32, out_ref.shape, 0)
    column = lax.broadcasted_iota(jnp.int32, out_ref.shape, 1)
    result = jnp.zeros(out_ref.shape, jnp.float32)
    for pair in range(pair_count):
        at = pair % 2
        r_real, r_imag = matrix(pair, 0)
        s_real, s_imag = matrix(pair, 1)
        sink = jnp.concatenate(
            [
                jnp.concatenate([s_real, -s_imag], 1),
                jnp.concatenate([s_imag, s_real], 1),
            ],
            0,
        )
        source = jnp.concatenate(
            [
                jnp.concatenate([r_real, r_imag], 1),
                jnp.concatenate([-r_imag, r_real], 1),
            ],
            0,
        )
        twice = jnp.concatenate([source, source], 0)
        for q in range(0, q_count, 2):
            pairwise = jnp.concatenate(
                [tau_ref[pair, q + i].reshape(2 * columns, columns) for i in range(2)], 1
            )
            halfway = dot(sink, pairwise)
            for i in range(2):
                rows = slice((q + i) * columns, (q + i + 1) * columns)
                for part in range(2):
                    value = halfway[
                        part * columns : (part + 1) * columns, i * columns : (i + 1) * columns
                    ]
                    high = value.astype(jnp.bfloat16)
                    low = (value - high.astype(jnp.float32)).astype(jnp.bfloat16)
                    h_ref[at, rows, part * columns : (part + 1) * columns] = high
                    h_ref[at, rows, (2 + part) * columns : (3 + part) * columns] = low
        for q in range(0, q_count, 4):
            rows = slice(q * columns, (q + 4) * columns)
            second_ref[at, rows] = dot(h_ref[at, rows], twice)
        sum_real = jnp.zeros((8, columns), jnp.float32)
        sum_imag = jnp.zeros((8, columns), jnp.float32)
        for q in range(q_count):
            spin_pair = where_ref[0] * q_count + q
            sign = jnp.where((spin_pair // 4 < 2) == (spin_pair % 4 < 2), 1.0, -1.0)
            part_real = jnp.zeros((8, columns), jnp.float32)
            part_imag = jnp.zeros((8, columns), jnp.float32)
            for start in range(0, columns, 16):
                rows = slice(q * columns + start, q * columns + start + 16)
                out_real = second_ref[at, rows, :columns]
                out_imag = second_ref[at, rows, columns:]
                tau_real = tau_ref[pair, q, 0, start : start + 16].astype(jnp.float32)
                tau_imag = tau_ref[pair, q, 1, start : start + 16].astype(jnp.float32)
                part_real += folded(out_real * tau_real + out_imag * tau_imag)
                part_imag += folded(out_imag * tau_real - out_real * tau_imag)
            sum_real += sign * part_real
            sum_imag += sign * part_imag
        total_real = jnp.sum(sum_real) / (4.0 * columns)
        total_imag = jnp.sum(sum_imag) / (4.0 * columns)
        result = jnp.where(column == pair, jnp.where(row == 0, total_real, total_imag), result)
    out_ref[...] = result


def elemental_kernel(where_ref, codes_ref, *refs):
    *halves, out_ref, table, rows_ref = refs
    fill(table, where_ref, [halves[i : i + 2] for i in range(0, len(halves), 2)])
    slices, slots, row_count = out_ref.shape[0], out_ref.shape[1], out_ref.shape[2]
    start = pl.multiple_of(where_ref[1] * row_count, row_count)
    for t in range(slices):
        for o in range(slots):
            real, imag = elemental(table, t ^ where_ref[0], codes_ref[o])
            rows_ref[0] = real
            rows_ref[1] = imag
            for part in range(2):
                out_ref[t, o, :, part] = rows_ref[part, pl.ds(start, row_count), :]


def shards(eigvecs, links, directions, pair_list, pair_operators, perambulators):
    slices, _, _, local_sites, columns = eigvecs.shape
    space = lax.axis_size("space")
    tm_size = lax.axis_size("tm")
    spin_size = lax.axis_size("spin")
    assert slices == spin_size and columns == LANES
    assert local_sites % (2 * PX * PY) == 0
    sites = PX * PY
    planes = local_sites // sites
    z_total = planes * space
    scale = 1.0 / math.sqrt(6.0 * sites * z_total)
    slots = directions.shape[0]
    pair_count, q_count = perambulators.shape[0], perambulators.shape[1]

    me = lax.axis_index("spin")
    layer = lax.axis_index("space")
    masks = []
    while 2 ** len(masks) < space:
        masks.append(2 ** len(masks))
    bits = [c % len(masks) for c in range(spin_size)]
    half_of = lambda core: (layer >> (core % len(masks))) & 1
    where = jnp.stack(
        [me, layer, lax.axis_index("tm"), spin_size, half_of(me), half_of(me ^ 1)]
    ).astype(jnp.int32)

    lowest = lax.dynamic_slice(eigvecs, (me, 0, 0, 0, 0), (1, 2, 3, sites, columns))[0]
    halo = lax.ppermute(lowest, "space", [(i, (i - 1) % space) for i in range(space)])
    halo, other_codes = lax.optimization_barrier((halo, flip(directions, "spin", 1)))
    codes = jnp.concatenate([directions, other_codes])

    params = pltpu.CompilerParams(dimension_semantics=("arbitrary",), vmem_limit_bytes=50 << 20)
    stack_shape = pltpu.VMEM((3 * sites, 2 * LANES), jnp.bfloat16)
    f_shape = pltpu.VMEM((4 * LANES, 3 * sites), jnp.bfloat16)
    vt_shape = pltpu.VMEM((6, LANES, sites), jnp.float32)
    link_field = pltpu.with_memory_space_constraint(
        links.transpose(0, 1, 3, 4, 2, 5), pltpu.MemorySpace.HBM
    )
    estimate = lambda flops: pl.CostEstimate(flops=flops, bytes_accessed=1 << 22, transcendentals=0)
    half_rows = columns // 2
    part_a, inner = pl.pallas_call(
        partial(plane_kernel, scale=scale, step=2.0 * math.pi / z_total),
        out_shape=(
            jax.ShapeDtypeStruct((2, 4, half_rows, columns), jnp.float32),
            jax.ShapeDtypeStruct((columns, columns), jnp.float32),
        ),
        grid_spec=pltpu.PrefetchScalarGridSpec(
            num_scalar_prefetch=1,
            grid=(planes // 2,),
            in_specs=[
                pl.BlockSpec((None, 2, 3, 2 * sites, columns), lambda z, w: (w[0], 0, 0, z, 0)),
                pl.BlockSpec((None, 3, 3, 3, 2, 2 * sites), lambda z, w: (w[0], 0, 0, 0, 0, z)),
                pl.BlockSpec(
                    (None, None, 3, 3, 2, sites),
                    lambda z, w: (w[0], 2, 0, 0, 0, jnp.maximum(2 * z - 1, 0)),
                ),
            ],
            out_specs=(
                pl.BlockSpec((2, 4, half_rows, columns), lambda z, w: (0, 0, 0, 0)),
                pl.BlockSpec((columns, columns), lambda z, w: (0, 0)),
            ),
            scratch_shapes=[
                pltpu.VMEM((2, columns, columns), jnp.float32),
                pltpu.VMEM((sites, sites), jnp.bfloat16),
                pltpu.VMEM((2, 6, LANES, sites), jnp.float32),
                pltpu.VMEM((2, 2 * LANES, 3 * sites), jnp.bfloat16),
                pltpu.VMEM((2, 3 * sites, 2 * LANES), jnp.bfloat16),
                pltpu.VMEM((2, 3 * sites, 2 * LANES), jnp.bfloat16),
                pltpu.VMEM((2, 3 * sites, 2 * LANES), jnp.bfloat16),
                pltpu.VMEM((2, 3, 3, 3, 3, sites), jnp.float32),
                pltpu.VMEM((2, 4 * LANES, 3 * sites), jnp.bfloat16),
                pltpu.VMEM((2, 4 * LANES, 3 * sites), jnp.bfloat16),
                pltpu.VMEM((2, 4 * LANES, 3 * sites), jnp.bfloat16),
                pltpu.VMEM((3, 2 * LANES, 2 * LANES), jnp.float32),
            ],
        ),
        compiler_params=pltpu.CompilerParams(
            dimension_semantics=("arbitrary",),
            vmem_limit_bytes=50 << 20,
        ),
        cost_estimate=estimate(20 * 10**9),
        name="planes",
    )(where, eigvecs, link_field, link_field)

    part_b = pl.pallas_call(
        partial(rim_kernel, scale=scale),
        out_shape=jax.ShapeDtypeStruct((2, 1, half_rows, columns), jnp.float32),
        grid_spec=pltpu.PrefetchScalarGridSpec(
            num_scalar_prefetch=1,
            grid=(1,),
            in_specs=[
                pl.BlockSpec((None, 2, 3, sites, columns), lambda z, w: (w[0], 0, 0, planes - 1, 0)),
                pl.BlockSpec(memory_space=pltpu.VMEM),
                pl.BlockSpec((None, None, 3, 3, 2, sites), lambda z, w: (w[0], 2, 0, 0, 0, planes - 1)),
                pl.BlockSpec(memory_space=pltpu.VMEM),
            ],
            out_specs=pl.BlockSpec((2, 1, half_rows, columns), lambda z, w: (0, 0, 0, 0)),
            scratch_shapes=[
                vt_shape,
                stack_shape,
                pltpu.VMEM((3, 3, 3, sites), jnp.float32),
                f_shape,
            ],
        ),
        compiler_params=params,
        cost_estimate=estimate(2 * 10**9),
        name="rim",
    )(where, eigvecs, halo, link_field, inner)

    sharing = [masks[bit] for bit in bits]
    got_a, got_b = flip_by_core(part_a[1], sharing), flip_by_core(part_b[1], sharing)
    small = pltpu.CompilerParams(vmem_limit_bytes=50 << 20)
    total = pl.pallas_call(
        join_kernel,
        out_shape=jax.ShapeDtypeStruct((5, half_rows, columns), jnp.float32),
        compiler_params=small,
        name="join",
    )(part_a, got_a, part_b, got_b)
    left = [[mask for mask in masks if mask != sharing[c]] for c in range(spin_size)]
    got = flip_by_core(total, [left[c][0] for c in range(spin_size)])
    for i in range(1, len(masks) - 1):
        total = total + got
        got = flip_by_core(total, [left[c][i] for c in range(spin_size)])

    mine = pl.pallas_call(
        round_kernel,
        out_shape=jax.ShapeDtypeStruct((5, half_rows, columns), jnp.bfloat16),
        compiler_params=small,
        name="round",
    )(total, got)
    own = [mine, flip_by_core(mine, sharing)]
    for m in range(1, tm_size):
        own += [flip_by_core(mine, [0] * spin_size, m), flip_by_core(mine, sharing, m)]
    other = [flip(half, "spin", 1) for half in own[:2]]

    resident = pl.BlockSpec(memory_space=pltpu.VMEM)
    whole = lambda shape: pl.BlockSpec(shape, lambda p, *_: (0,) * len(shape))

    row_count = columns // space
    elementals = pl.pallas_call(
        elemental_kernel,
        out_shape=jax.ShapeDtypeStruct((slices, slots, row_count, 2, columns), jnp.float32),
        grid_spec=pltpu.PrefetchScalarGridSpec(
            num_scalar_prefetch=2,
            grid=(1,),
            in_specs=[resident] * 4,
            out_specs=whole((slices, slots, row_count, 2, columns)),
            scratch_shapes=[
                pltpu.VMEM((spin_size, 5, columns, columns), jnp.bfloat16),
                pltpu.VMEM((2, columns, columns), jnp.float32),
            ],
        ),
        compiler_params=params,
        name="rows",
    )(where, codes, *own[:2], *other)
    *rest, elementals = lax.optimization_barrier((*own[2:], elementals))
    own = own[:2] + rest
    other = other + [flip(half, "spin", 1) for half in rest]

    partial_corr = pl.pallas_call(
        partial(pair_kernel, tm_size=tm_size, slots=slots),
        out_shape=jax.ShapeDtypeStruct((2, pair_count), jnp.float32),
        grid_spec=pltpu.PrefetchScalarGridSpec(
            num_scalar_prefetch=4,
            grid=(1,),
            in_specs=[resident] * (2 * len(own) + 1),
            out_specs=whole((2, pair_count)),
            scratch_shapes=[
                pltpu.VMEM((spin_size * tm_size, 5, columns, columns), jnp.bfloat16),
                pltpu.VMEM((2, q_count * columns, 4 * columns), jnp.bfloat16),
                pltpu.VMEM((2, q_count * columns, 2 * columns), jnp.float32),
            ],
        ),
        compiler_params=params,
        name="pairs",
    )(where, codes, pair_list.T, pair_operators.T, *own, *other, perambulators)
    correlators = (partial_corr + flip(partial_corr, "spin", 1)).T

    return elementals, correlators


def solution(mesh):
    return jax.shard_map(
        shards,
        mesh=mesh,
        in_specs=(
            P("tm", None, None, "space", None),
            P("tm", None, None, None, None, "space"),
            P("spin"),
            P(("space", "tm"), None),
            P(("space", "tm"), None),
            P(("space", "tm"), "spin", None, None, None),
        ),
        out_specs=(P(("ens", "tm"), "spin", "space", None, None), P(("ens", "space", "tm"), None)),
        check_vma=False,
    )
```
